128 devices in a mesh: ctx: 8 (over x, y_lo), ffn: 16 (over z, y_hi, core).
Axes of the slice: x: 4, y: 4 (y_hi: 2, y_lo: 2; y = y_hi * 2 + y_lo), z: 4, core: 2. Of those that a mesh axis runs over, the one named last changes fastest.
Arguments:
- resid_in: bfloat16 [1024, 4096], P(('ctx', 'ffn')), may hold values from -6 to 6
- queries: bfloat16 [1024, 4096], P('ctx', 'ffn'), may hold values from -6 to 6
- keys_in: bfloat16 [1024, 1024], P('ctx'), may hold values from -6 to 6
- value_rows_input: bfloat16 [1024, 1024], P('ctx'), may hold values from -6 to 6
- w_out: bfloat16 [4096, 4096], P('ffn'), may hold values from -0.09375 to 0.09375
- norm_gain: float32 [4096], replicated, may hold values from 0.5 to 1.5
- w_gate: bfloat16 [4096, 7168], P(None, 'ffn'), may hold values from -0.09375 to 0.09375
- w_up: bfloat16 [4096, 7168], P(None, 'ffn'), may hold values from -0.09375 to 0.09375
- w_down: bfloat16 [7168, 4096], P('ffn'), may hold values from -0.0625 to 0.0625
- cotangent: bfloat16 [1024, 4096], P(('ctx', 'ffn')), may hold values from -6 to 6
- positions: int32 [1024], P('ctx'), may hold values from 0 to 1023, as said below
- doc_ids: int32 [1024], replicated, may hold values from 0 to 3, never falling along the last dimension, each value on 1 to 512 neighbouring positions
Outputs:
- mixed: bfloat16 [1024, 4096], P(('ctx', 'ffn'))
- grad_resid: bfloat16 [1024, 4096], P(('ctx', 'ffn'))
- grad_queries: bfloat16 [1024, 4096], P('ctx', 'ffn')
- key_gradient_rows: float32 [1024, 1024], P(('ctx', 'ffn'))
- value_gradient_rows: float32 [1024, 1024], P(('ctx', 'ffn'))
- grad_gain: float32 [4096], replicated
- grad_w_out: float32 [4096, 4096], P('ffn', 'ctx')
- grad_w_gate: float32 [4096, 7168], P('ctx', 'ffn')
- grad_w_up: float32 [4096, 7168], P('ctx', 'ffn')
- grad_w_down: float32 [7168, 4096], P('ffn', 'ctx')
The draws below stay inside these ranges and needn't reach their ends.
Inputs may be any that keep to these rules, and one draw needn't show every extreme that they name: Each aligned block of 64 rows holds 64 consecutive positions in rising order, and every position occurs once.
All inputs are finite; a program needn't handle non-finite values.
Results may differ from the reference program's by a relative error of at most 0.033.
Values may be sent and summed in bfloat16 or wider, within the bound.
A program may use at most 128 MiB of HBM per device.

```python
import math
import jax
import jax.numpy as jnp
import numpy as np
from jax import lax

D = 4096
QUERY_HEADS = 32
KEY_VALUE_HEADS = 8
HEAD_WIDTH = 128
FF = 7168
STRIPE = 64
TOKEN_COUNT = 1024


def draw_queries(key, part):
    sampled_draw = jnp.clip(jax.random.normal(jax.random.fold_in(key, 3), (TOKEN_COUNT, QUERY_HEADS * HEAD_WIDTH), jnp.float32), -6.0, 6.0)
    return sampled_draw.astype(jnp.bfloat16)


def draw_keys_in(key, part):
    sampled_draw = jnp.clip(jax.random.normal(jax.random.fold_in(key, 5), (TOKEN_COUNT, KEY_VALUE_HEADS * HEAD_WIDTH), jnp.float32), -6.0, 6.0)
    return sampled_draw.astype(jnp.bfloat16)


def draw_positions(key, part):
    block_order = jax.random.permutation(jax.random.fold_in(key, 9), TOKEN_COUNT // STRIPE)
    within = jnp.arange(STRIPE)
    return (block_order[:, None] * STRIPE + within[None, :]).reshape(TOKEN_COUNT).astype(jnp.int32)


def levels(own_key, extent, shards, low, largest):
    def one(position, blocks):
        heights = jax.random.uniform(jax.random.fold_in(jax.random.fold_in(own_key, 6), position), (blocks,), jnp.float32, low / len(shards), largest / len(shards))
        return jnp.repeat(jnp.exp(heights), extent[position] // blocks).reshape((-1,) + (1,) * (len(extent) - position - 1))

    level = one(*shards[0])
    for cut in shards[1:]:
        level = level * one(*cut)
    return level


def profile(count, total, bound, lean):
    portions = [(1 << 20) // math.isqrt(standing ** lean) + 1 for standing in range(2, count + 1)]
    spare, given = total - bound - (count - 1), [1] * (count - 1)
    while spare > 0:
        candidates = [i for i in range(count - 1) if given[i] < bound]
        mass, left = sum([portions[i] for i in candidates]), spare
        for i in candidates:
            extra = min(bound - given[i], max(1, left * portions[i] // mass), spare)
            given[i] = given[i] + extra
            spare = spare - extra
    return np.array([bound] + given)


def uneven(stream_key, count, total, most, skew):
    if count == 2:
        one = jax.random.randint(stream_key, (), max(1, total - most), min(most, total - 1) + 1)
        return jnp.stack([one, total - one])
    sizes = jnp.asarray(profile(count, total, most, skew), jnp.int32)
    pairs = (count - 1) // 2
    source_of, receiver = sizes[1:1 + 2 * pairs:2], sizes[2:2 + 2 * pairs:2]
    slack = jnp.minimum(source_of - 1, most - receiver)
    moved = jax.random.randint(jax.random.fold_in(stream_key, 1), (pairs,), 0, 1 << 20) % (slack + 1)
    sizes = sizes.at[1:1 + 2 * pairs:2].set(source_of - moved).at[2:2 + 2 * pairs:2].set(receiver + moved)
    return sizes[jax.random.permutation(jax.random.fold_in(stream_key, 2), count)]


def gaussian(own_key, shape, scale, reach, split=(), kind=jnp.bfloat16):
    factor_of = levels(own_key, shape, split, -0.22, 0.18) if split else 1.0
    array = jax.random.normal(own_key, shape, jnp.float32) * scale * factor_of
    return jnp.minimum(jnp.maximum(array, -reach), reach).astype(kind)


def setup_inputs(seed: int = 0) -> dict:
    streams_of = jax.random.split(jax.random.key(seed), 13)
    resid_in = gaussian(streams_of[0], (TOKEN_COUNT, D), 1.0, 6.0, ((0, 128),))
    queries = draw_queries(jax.random.fold_in(streams_of[12], 71), 0)
    keys_in = draw_keys_in(jax.random.fold_in(streams_of[12], 71), 0)
    value_rows_input = gaussian(streams_of[3], (TOKEN_COUNT, KEY_VALUE_HEADS * HEAD_WIDTH), 1.0, 6.0, ((0, 8),))
    w_out = gaussian(streams_of[4], (QUERY_HEADS * HEAD_WIDTH, D), (QUERY_HEADS * HEAD_WIDTH) ** -0.5, 0.09375, ((0, 16),))
    norm_gain = jnp.clip(1.0 + 0.1 * jax.random.normal(streams_of[5], (D,), jnp.float32), 0.5, 1.5)
    w_gate = gaussian(streams_of[6], (D, FF), D ** -0.5, 0.09375, ((1, 16),))
    w_up = gaussian(streams_of[7], (D, FF), D ** -0.5, 0.09375, ((1, 16),))
    w_down = gaussian(streams_of[8], (FF, D), FF ** -0.5, 0.0625, ((0, 16),))
    cotangent = gaussian(streams_of[9], (TOKEN_COUNT, D), 1.0, 6.0, ((0, 128),))
    positions = draw_positions(jax.random.fold_in(streams_of[12], 71), 0)
    doc_ids = jnp.searchsorted(jnp.cumsum(uneven(streams_of[11], 4, TOKEN_COUNT, TOKEN_COUNT // 2, 0)), jnp.arange(TOKEN_COUNT), side="right").astype(jnp.int32)
    return dict(resid_in=resid_in, queries=queries, keys_in=keys_in, value_rows_input=value_rows_input, w_out=w_out, norm_gain=norm_gain, w_gate=w_gate, w_up=w_up, w_down=w_down, cotangent=cotangent, positions=positions, doc_ids=doc_ids)


masked_fill = -1e+30
norm_eps = 1e-05

def head_slices(queries, keys_in, value_rows_input, query_head_index):
    key_value_index = query_head_index // (QUERY_HEADS // KEY_VALUE_HEADS)
    return (lax.dynamic_slice_in_dim(queries, query_head_index * HEAD_WIDTH, HEAD_WIDTH, 1), lax.dynamic_slice_in_dim(keys_in, key_value_index * HEAD_WIDTH, HEAD_WIDTH, 1), lax.dynamic_slice_in_dim(value_rows_input, key_value_index * HEAD_WIDTH, HEAD_WIDTH, 1))

def masked_scores(q_head, k_head, visible):
    scores = jnp.dot(q_head, k_head.T, preferred_element_type=jnp.float32) * (1.0 / math.sqrt(HEAD_WIDTH))
    return jnp.where(visible, scores, masked_fill)

def attention_forward(queries, keys_in, value_rows_input, visible):

    def one_head(query_head_index):
        q_head, k_head, v_head = head_slices(queries, keys_in, value_rows_input, query_head_index)
        scores = masked_scores(q_head, k_head, visible)
        row_max = lax.optimization_barrier(jnp.max(scores, axis=1, keepdims=True))
        weights = jnp.where(visible, jnp.exp(scores - row_max), 0.0)
        row_total = lax.optimization_barrier(jnp.sum(weights, axis=1, keepdims=True))
        output = jnp.dot(weights.astype(jnp.bfloat16), v_head, preferred_element_type=jnp.float32) / row_total
        return (output.astype(jnp.bfloat16), (row_max + jnp.log(row_total))[:, 0])
    return lax.map(one_head, jnp.arange(QUERY_HEADS, dtype=jnp.int32))

def attention_backward(queries, keys_in, value_rows_input, grad_attended, log_totals, deltas, visible):
    scale_value = 1.0 / math.sqrt(HEAD_WIDTH)

    def one_head(query_head_index):
        q_head, k_head, v_head = head_slices(queries, keys_in, value_rows_input, query_head_index)
        g_head = lax.dynamic_slice_in_dim(grad_attended, query_head_index * HEAD_WIDTH, HEAD_WIDTH, 1)
        scores = masked_scores(q_head, k_head, visible)
        prob_weights = jnp.where(visible, jnp.exp(scores - log_totals[query_head_index][:, None]), 0.0)
        grad_probs = jnp.dot(g_head, v_head.T, preferred_element_type=jnp.float32)
        grad_scores = (prob_weights * (grad_probs - deltas[query_head_index][:, None])).astype(jnp.bfloat16)
        grad_q = jnp.dot(grad_scores, k_head, preferred_element_type=jnp.float32) * scale_value
        grad_k = jnp.dot(grad_scores.T, q_head, preferred_element_type=jnp.float32) * scale_value
        grad_v = jnp.dot(prob_weights.astype(jnp.bfloat16).T, g_head, preferred_element_type=jnp.float32)
        return (grad_q.astype(jnp.bfloat16), grad_k, grad_v)
    return lax.map(one_head, jnp.arange(QUERY_HEADS, dtype=jnp.int32))

def group_sum(pairs):
    total_sum = jnp.zeros((pairs[0][0].shape[0], pairs[0][1].shape[1]), jnp.float32)
    for left, right in pairs:
        total_sum = total_sum + jnp.dot(left, right, preferred_element_type=jnp.float32)
    return total_sum

def block_sum(left_rows, right_rows):
    return jnp.dot(left_rows.T, right_rows, preferred_element_type=jnp.float32)

def reference(resid_in, queries, keys_in, value_rows_input, w_out, norm_gain, w_gate, w_up, w_down, cotangent, positions, doc_ids):
    seg_rows = doc_ids[positions]
    visible = (positions[None, :] <= positions[:, None]) & (seg_rows[None, :] == seg_rows[:, None])
    head_out, log_totals = attention_forward(queries, keys_in, value_rows_input, visible)
    attended = jnp.transpose(head_out, (1, 0, 2)).reshape(TOKEN_COUNT, QUERY_HEADS * HEAD_WIDTH)
    hidden_bf = (resid_in.astype(jnp.float32) + group_sum([(attended, w_out)])).astype(jnp.bfloat16)
    hidden_f = lax.optimization_barrier(hidden_bf).astype(jnp.float32)
    inv_rms = lax.rsqrt(lax.optimization_barrier(jnp.mean(hidden_f * hidden_f, axis=1, keepdims=True)) + norm_eps)
    normed = (hidden_f * inv_rms * norm_gain).astype(jnp.bfloat16)
    gate_pre = jnp.dot(normed, w_gate, preferred_element_type=jnp.float32)
    up_proj = jnp.dot(normed, w_up, preferred_element_type=jnp.float32)
    gate_sig = jax.nn.sigmoid(gate_pre)
    activated = (gate_pre * gate_sig * up_proj).astype(jnp.bfloat16)
    mixed = (hidden_f + group_sum([(activated, w_down)])).astype(jnp.bfloat16)
    grad_act = jnp.dot(cotangent, w_down.T, preferred_element_type=jnp.float32)
    grad_up = (grad_act * gate_pre * gate_sig).astype(jnp.bfloat16)
    grad_gate = (grad_act * up_proj * gate_sig * (1.0 + gate_pre * (1.0 - gate_sig))).astype(jnp.bfloat16)
    grad_normed = group_sum([(grad_gate, w_gate.T), (grad_up, w_up.T)])
    gained = grad_normed * norm_gain
    inv_cube = inv_rms * inv_rms * inv_rms
    grad_resid = (cotangent.astype(jnp.float32) + inv_rms * gained - hidden_f * inv_cube * lax.optimization_barrier(jnp.mean(gained * hidden_f, axis=1, keepdims=True))).astype(jnp.bfloat16)
    grad_gain = lax.optimization_barrier(jnp.sum(grad_normed * hidden_f * inv_rms, axis=0))
    grad_attended = jnp.dot(grad_resid, w_out.T, preferred_element_type=jnp.float32).astype(jnp.bfloat16)
    deltas = lax.optimization_barrier(jnp.sum((grad_attended.astype(jnp.float32) * attended.astype(jnp.float32)).reshape(TOKEN_COUNT, QUERY_HEADS, HEAD_WIDTH), axis=2)).T
    grad_q_heads, key_head_gradient, value_head_gradient = attention_backward(queries, keys_in, value_rows_input, grad_attended, log_totals, deltas, visible)
    grad_queries = jnp.transpose(grad_q_heads, (1, 0, 2)).reshape(TOKEN_COUNT, QUERY_HEADS * HEAD_WIDTH)
    heads_per_group = QUERY_HEADS // KEY_VALUE_HEADS
    key_gradient_rows = jnp.transpose(key_head_gradient.reshape(KEY_VALUE_HEADS, heads_per_group, TOKEN_COUNT, HEAD_WIDTH).sum(axis=1), (1, 0, 2)).reshape(TOKEN_COUNT, KEY_VALUE_HEADS * HEAD_WIDTH)
    value_gradient_rows = jnp.transpose(value_head_gradient.reshape(KEY_VALUE_HEADS, heads_per_group, TOKEN_COUNT, HEAD_WIDTH).sum(axis=1), (1, 0, 2)).reshape(TOKEN_COUNT, KEY_VALUE_HEADS * HEAD_WIDTH)
    grad_w_out = block_sum(attended, grad_resid)
    grad_w_gate = block_sum(normed, grad_gate)
    grad_w_up = block_sum(normed, grad_up)
    grad_w_down = block_sum(activated, cotangent)
    return (mixed, grad_resid, grad_queries, key_gradient_rows, value_gradient_rows, grad_gain, grad_w_out, grad_w_gate, grad_w_up, grad_w_down)
```

```python
import functools
import math

import jax
import jax.numpy as jnp
from jax import lax
from jax.experimental import pallas as pl
from jax.experimental.pallas import tpu as pltpu
from jax.sharding import PartitionSpec as P

MESH = pl.DeviceIdType.MESH
F32 = jnp.float32
BF = jnp.bfloat16
CTX = 8
CHIPS = 8
HW = 128
SCALE = 1.0 / math.sqrt(128)
NEG = -1e30
EPS = 1e-05
NT = (((1,), (1,)), ((), ()))


class Net:
    def __init__(self, ssem, rsem):
        self.ssem, self.rsem, self.used = ssem, rsem, 0
        self.c = lax.axis_index("ctx")
        self.f = lax.axis_index("ffn")
        self.core = lax.rem(self.f, 2)
        self.chip = self.f // 2
        self.partner = self.f + 1 - 2 * self.core

    def copy(self, src, dst, c=None, f=None):
        n = self.used
        self.used = n + 1
        return pltpu.make_async_remote_copy(
            src_ref=src,
            dst_ref=dst,
            send_sem=self.ssem.at[n],
            recv_sem=self.rsem.at[n],
            device_id=(self.c if c is None else c, self.f if f is None else f),
            device_id_type=MESH,
        )

    def ctx_to(self, k):
        return lax.rem(self.c + k, CTX)

    def ctx_from(self, k):
        return lax.rem(self.c + CTX - k, CTX)

    def chip_to(self, k):
        return lax.rem(self.chip + k, CHIPS)

    def chip_from(self, k):
        return lax.rem(self.chip + CHIPS - k, CHIPS)

    def greet(self, all_ffn):
        barrier = pltpu.get_barrier_semaphore()
        count = 0
        for k in range(1, CTX):
            pl.semaphore_signal(
                barrier, inc=1, device_id=(self.ctx_to(k), self.f), device_id_type=MESH
            )
            count += 1
        if all_ffn:
            for k in range(1, 16):
                pl.semaphore_signal(
                    barrier,
                    inc=1,
                    device_id=(self.c, lax.rem(self.f + k, 16)),
                    device_id_type=MESH,
                )
                count += 1
        else:
            for k in range(1, CHIPS):
                pl.semaphore_signal(
                    barrier,
                    inc=1,
                    device_id=(self.c, self.chip_to(k) * 2 + self.core),
                    device_id_type=MESH,
                )
                count += 1
            pl.semaphore_signal(
                barrier, inc=1, device_id=(self.c, self.partner), device_id_type=MESH
            )
            count += 1
        pl.semaphore_wait(barrier, count)


def ctx_gather(net, src, dst):
    return [net.copy(src, dst.at[net.c], c=net.ctx_to(k)) for k in range(1, CTX)]


def ctx_columns(net, src, dst):
    out = []
    for k in range(1, CTX):
        to = net.ctx_to(k)
        cols = pl.ds(pl.multiple_of(to * 512, 512), 512)
        out.append(net.copy(src.at[:, :, cols], dst.at[net.c], c=to))
    return out


class FfnGather:
    def __init__(self, net, src, dst):
        self.net, self.dst = net, dst
        self.far = [
            net.copy(src, dst.at[net.f], f=net.chip_to(k) * 2 + net.core) for k in range(1, CHIPS)
        ]
        self.near = [net.copy(src, dst.at[net.f], f=net.partner)]

    def start(self):
        for cp in self.far:
            cp.start()
        self.near[0].start()

    def forward(self):
        net = self.net
        for k in range(1, CHIPS):
            self.far[k - 1].wait_recv()
            block = self.dst.at[net.chip_from(k) * 2 + net.core]
            cp = net.copy(block, block, f=net.partner)
            cp.start()
            self.near.append(cp)

    def finish(self):
        for cp in self.near:
            cp.wait_recv()

    def drain(self):
        for cp in self.far + self.near:
            cp.wait_send()


class FfnScatter:
    def __init__(self, net, part, pair_in, summed, got):
        self.net, self.part, self.pair_in, self.summed, self.got = net, part, pair_in, summed, got
        self.pair = net.copy(part.at[:, 1 - net.core], pair_in, f=net.partner)
        self.far = [
            net.copy(
                summed.at[net.chip_to(k)],
                got.at[net.chip],
                f=net.chip_to(k) * 2 + net.core,
            )
            for k in range(1, CHIPS)
        ]

    def start(self):
        self.pair.start()

    def chip_sum(self, to):
        return self.part[to, self.net.core].astype(F32) + self.pair_in[to].astype(F32)

    def middle(self):
        net = self.net
        self.pair.wait_recv()
        for k in range(1, CHIPS):
            to = net.chip_to(k)
            self.summed[to] = self.chip_sum(to).astype(BF)
            self.far[k - 1].start()

    def finish(self):
        net = self.net
        total = self.chip_sum(net.chip)
        for k in range(1, CHIPS):
            self.far[k - 1].wait_recv()
            total = total + self.got[net.chip_from(k)].astype(F32)
        return total

    def drain(self):
        self.pair.wait_send()
        for cp in self.far:
            cp.wait_send()


def seg_starts(doc_ref, pos):
    doc = doc_ref[...]
    start = jnp.zeros_like(pos)
    for v in (1, 2, 3):
        edge = jnp.sum((doc < v).astype(F32))
        start = jnp.where(pos >= edge, jnp.maximum(start, edge), start)
    return start


def as_column(row):
    return jnp.transpose(jnp.broadcast_to(row, (128, 128)))


def as_row(column):
    return jnp.transpose(jnp.broadcast_to(column, (128, 128)))[0:1, :]


def front(
    keys, values, q, pos, doc, wout, resid, gain, cot,
    att, lse, k_all, v_all, q_all, pos_all, hid, inv, nrm_all, cot_all,
    part, pair_in, summed, got, nbuf, ssem, rsem,
):
    net = Net(ssem, rsem)
    c, f = net.c, net.f
    net.greet(False)
    cols = pl.ds(pl.multiple_of(net.chip * 128, 128), 128)
    first = (
        ctx_gather(net, keys.at[:, cols], k_all)
        + ctx_gather(net, values.at[:, cols], v_all)
        + ctx_gather(net, pos, pos_all)
    )
    for cp in first:
        cp.start()
    k_all[c] = keys[:, cols]
    v_all[c] = values[:, cols]
    pos_all[c] = pos[...]
    q_all[c] = q[...]
    cot_all[f] = cot[...]
    cot_gather = FfnGather(net, cot, cot_all)
    q_gather = ctx_gather(net, q, q_all)
    for cp in first:
        cp.wait_recv()
    cot_gather.start()
    for cp in q_gather:
        cp.start()
    kpos = jnp.concatenate([pos_all[i] for i in range(CTX)], axis=1)
    qpos = as_column(pos[...])[:, 0:1]
    qstart = seg_starts(doc, qpos)
    visible = (kpos <= qpos) & (kpos >= qstart)
    k = k_all[...].reshape(1024, 128)
    v = v_all[...].reshape(1024, 128)
    rows = []
    for h in range(2):
        qh = q[:, h * 128 : (h + 1) * 128]
        s = lax.dot_general(qh, k, NT, preferred_element_type=F32) * SCALE
        s = jnp.where(visible, s, NEG)
        top = jnp.max(s, axis=1, keepdims=True)
        w = jnp.where(visible, jnp.exp(s - top), 0.0)
        total = jnp.sum(w, axis=1, keepdims=True)
        o = jnp.dot(w.astype(BF), v, preferred_element_type=F32) / total
        att[:, h * 128 : (h + 1) * 128] = o.astype(BF)
        rows.append(as_row(top + jnp.log(total)))
    lse[...] = jnp.concatenate(rows + [jnp.zeros((6, 128), F32)], axis=0)
    a = att[...]
    for n in range(8):
        span = slice(n * 512, (n + 1) * 512)
        r = jnp.dot(a, wout[:, span], preferred_element_type=F32)
        for b in range(16):
            part[b // 2, b % 2, :, span] = r[b * 8 : (b + 1) * 8].astype(BF)
    rs = FfnScatter(net, part, pair_in, summed, got)
    rs.start()
    rs.middle()
    cot_gather.forward()
    projected = rs.finish()
    hidden = (resid[...].astype(F32) + projected).astype(BF)
    hid[...] = hidden
    hf = hidden.astype(F32)
    ir = lax.rsqrt(jnp.mean(hf * hf, axis=1, keepdims=True) + EPS)
    inv[...] = jnp.broadcast_to(ir, (8, 128))
    normed = (hf * ir * gain[...]).astype(BF)
    nbuf[...] = normed
    nrm_all[f] = normed
    ag = FfnGather(net, nbuf, nrm_all)
    ag.start()
    cot_gather.finish()
    ag.forward()
    ag.finish()
    for cp in q_gather:
        cp.wait_recv()
    for cp in first + q_gather:
        cp.wait_send()
    cot_gather.drain()
    rs.drain()
    ag.drain()


def back(
    gn, mx, hid, inv, cot, gain, nrm_all, cot_all, gu, act, att, wout, q, q_all, k_all, v_all,
    pos_all, doc, lse,
    mixed, gres, dq, kg, vg, gg, nrm_c, cot_c, gres_c, gu_all, act_all, att_all,
    pair_in, summed, got, pair_in2, summed2, got2, gbuf, grows, ga, ga_all, stats, stats_all,
    kv, kv_in, gsum, gpair, gchip, gctx_b, gctx, ssem, rsem,
):
    net = Net(ssem, rsem)
    c, f = net.c, net.f
    net.greet(True)
    rs = FfnScatter(net, gn, pair_in, summed, got)
    rs2 = FfnScatter(net, mx, pair_in2, summed2, got2)
    rs.start()
    rs2.start()
    rs.middle()
    bulk = (
        ctx_gather(net, att, att_all)
        + ctx_gather(net, gu, gu_all)
        + ctx_gather(net, act, act_all)
        + ctx_columns(net, nrm_all, nrm_c)
        + ctx_columns(net, cot_all, cot_c)
    )
    for cp in bulk:
        cp.start()
    own = pl.ds(pl.multiple_of(c * 512, 512), 512)
    att_all[c] = att[...]
    gu_all[c] = gu[...]
    act_all[c] = act[...]
    nrm_c[c] = nrm_all[:, :, own]
    cot_c[c] = cot_all[:, :, own]
    gnorm = rs.finish()
    hf = hid[...].astype(F32)
    ir = inv[:, 0:1]
    gained = gnorm * gain[...]
    cube = ir * ir * ir
    mean = jnp.mean(gained * hf, axis=1, keepdims=True)
    gr = (cot[...].astype(F32) + ir * gained - hf * cube * mean).astype(BF)
    gres[...] = gr
    gbuf[...] = gr
    grows[f] = gr
    gsum[...] = jnp.sum(gnorm * hf * ir, axis=0, keepdims=True)
    ag = FfnGather(net, gbuf, grows)
    ag.start()
    g1 = net.copy(gsum, gpair, f=net.partner)
    g1.start()
    rs2.middle()
    g1.wait_recv()
    gchip[net.chip] = gsum[...] + gpair[...]
    g2 = [
        net.copy(gchip.at[net.chip], gchip.at[net.chip], f=net.chip_to(k_) * 2 + net.core)
        for k_ in range(1, CHIPS)
    ]
    for cp in g2:
        cp.start()
    ag.forward()
    ag.finish()
    rows = jnp.concatenate([grows[b] for b in range(16)], axis=0)
    gat = lax.dot_general(rows, wout[...], NT, preferred_element_type=F32).astype(BF)
    ga[...] = gat
    ga_all[c] = gat
    prod = gat.astype(F32) * att[...].astype(F32)
    delta = [jnp.sum(prod[:, h * 128 : (h + 1) * 128], axis=1, keepdims=True) for h in range(2)]
    st = jnp.concatenate(
        [lse[0:2, :], as_row(delta[0]), as_row(delta[1]), jnp.zeros((4, 128), F32)], axis=0
    )
    stats[...] = st
    stats_all[c] = st
    late = ctx_gather(net, ga, ga_all) + ctx_gather(net, stats, stats_all)
    for cp in late:
        cp.start()
    late2 = ctx_columns(net, grows, gres_c)
    for cp in late2:
        cp.start()
    gres_c[c] = grows[:, :, own]
    kpos = jnp.concatenate([pos_all[i] for i in range(CTX)], axis=1)
    mypos = pos_all[c]
    qpos = as_column(mypos)[:, 0:1]
    visible = (kpos <= qpos) & (kpos >= seg_starts(doc, qpos))
    k = k_all[...].reshape(1024, 128)
    v = v_all[...].reshape(1024, 128)
    for h in range(2):
        hs = slice(h * 128, (h + 1) * 128)
        s = lax.dot_general(q[:, hs], k, NT, preferred_element_type=F32) * SCALE
        lcol = as_column(lse[h : h + 1, :])[:, 0:1]
        p = jnp.where(visible, jnp.exp(jnp.where(visible, s, NEG) - lcol), 0.0)
        dp = lax.dot_general(gat[:, hs], v, NT, preferred_element_type=F32)
        ds = (p * (dp - delta[h])).astype(BF)
        dq[:, hs] = (jnp.dot(ds, k, preferred_element_type=F32) * SCALE).astype(BF)
    for cp in g2:
        cp.wait_recv()
    tot = gchip[0]
    for i in range(1, CHIPS):
        tot = tot + gchip[i]
    gctx_b[...] = tot
    gctx[c] = tot
    g3 = ctx_gather(net, gctx_b, gctx)
    for cp in g3:
        cp.start()
    mixed[...] = (hf + rs2.finish()).astype(BF)
    for cp in late:
        cp.wait_recv()
    qrow = kpos
    qs = seg_starts(doc, kpos)
    vis_t = (qpos <= qrow) & (qpos >= qs)
    k_own = k_all[c]
    v_own = v_all[c]
    dk = jnp.zeros((128, 128), F32)
    dv = jnp.zeros((128, 128), F32)
    for h in range(2):
        hs = slice(h * 128, (h + 1) * 128)
        qa = q_all[:, :, hs].reshape(1024, 128)
        gaa = ga_all[:, :, hs].reshape(1024, 128)
        lrow = jnp.concatenate([stats_all[i, h : h + 1, :] for i in range(CTX)], axis=1)
        drow = jnp.concatenate([stats_all[i, 2 + h : 3 + h, :] for i in range(CTX)], axis=1)
        s = lax.dot_general(k_own, qa, NT, preferred_element_type=F32) * SCALE
        p = jnp.where(vis_t, jnp.exp(jnp.where(vis_t, s, NEG) - lrow), 0.0)
        dp = lax.dot_general(v_own, gaa, NT, preferred_element_type=F32)
        ds = (p * (dp - drow)).astype(BF)
        dk = dk + jnp.dot(ds, qa, preferred_element_type=F32)
        dv = dv + jnp.dot(p.astype(BF), gaa, preferred_element_type=F32)
    dkv = jnp.concatenate([dk * SCALE, dv], axis=1)
    for b in range(16):
        kv[b] = dkv[b * 8 : (b + 1) * 8]
    kv_in[f] = kv[f]
    last = []
    for n in range(1, 16):
        to = lax.rem(f + n, 16)
        last.append(net.copy(kv.at[to], kv_in.at[f], f=to))
    for cp in last:
        cp.start()
    for cp in g3:
        cp.wait_recv()
    tot = gctx[0]
    for i in range(1, CTX):
        tot = tot + gctx[i]
    gg[...] = tot
    for cp in last:
        cp.wait_recv()
    for g in range(8):
        pair = kv_in[2 * g] + kv_in[2 * g + 1]
        kg[:, g * 128 : (g + 1) * 128] = pair[:, 0:128]
        vg[:, g * 128 : (g + 1) * 128] = pair[:, 128:256]
    for cp in bulk + late2:
        cp.wait_recv()
    for cp in bulk + late + late2 + g2 + g3 + last + [g1]:
        cp.wait_send()
    rs.drain()
    rs2.drain()
    ag.drain()


VM = pl.BlockSpec(memory_space=pltpu.VMEM)


def call(kernel, outs, scratch, sems, collective_id, args):
    return pl.pallas_call(
        kernel,
        out_shape=[jax.ShapeDtypeStruct(s, d) for s, d in outs],
        in_specs=[VM] * len(args),
        out_specs=[VM] * len(outs),
        scratch_shapes=[pltpu.VMEM(s, d) for s, d in scratch]
        + [pltpu.SemaphoreType.DMA((sems,)), pltpu.SemaphoreType.DMA((sems,))],
        compiler_params=pltpu.CompilerParams(
            collective_id=collective_id, has_side_effects=True, vmem_limit_bytes=60 * 2**20
        ),
    )(*args)


def body(
    resid_in, queries, keys_in, value_rows_input, w_out, norm_gain, w_gate, w_up, w_down,
    cotangent, positions, doc_ids,
):
    pos = positions.astype(F32).reshape(1, 128)
    doc = doc_ids.reshape(8, 128)
    gain = norm_gain.reshape(1, 4096)
    att, lse, k_all, v_all, q_all, pos_all, hid, inv, nrm_all, cot_all = call(
        front,
        [
            ((128, 256), BF),
            ((8, 128), F32),
            ((8, 128, 128), BF),
            ((8, 128, 128), BF),
            ((8, 128, 256), BF),
            ((8, 1, 128), F32),
            ((8, 4096), BF),
            ((8, 128), F32),
            ((16, 8, 4096), BF),
            ((16, 8, 4096), BF),
        ],
        [
            ((8, 2, 8, 4096), BF),
            ((8, 8, 4096), BF),
            ((8, 8, 4096), BF),
            ((8, 8, 4096), BF),
            ((8, 4096), BF),
        ],
        80,
        0,
        (keys_in, value_rows_input, queries, pos, doc, w_out, resid_in, gain, cotangent),
    )
    normed_rows = nrm_all.reshape(128, 4096)
    cot_rows = cot_all.reshape(128, 4096)
    gate_pre = jnp.dot(normed_rows, w_gate, preferred_element_type=F32)
    up_proj = jnp.dot(normed_rows, w_up, preferred_element_type=F32)
    sig = jax.nn.sigmoid(gate_pre)
    activated = (gate_pre * sig * up_proj).astype(BF)
    mx = jnp.dot(activated, w_down, preferred_element_type=F32).astype(BF)
    grad_act = jnp.dot(cot_rows, w_down.T, preferred_element_type=F32)
    grad_up = (grad_act * gate_pre * sig).astype(BF)
    grad_gate = (grad_act * up_proj * sig * (1.0 + gate_pre * (1.0 - sig))).astype(BF)
    gn = (
        jnp.dot(grad_gate, w_gate.T, preferred_element_type=F32)
        + jnp.dot(grad_up, w_up.T, preferred_element_type=F32)
    ).astype(BF)
    gu = jnp.concatenate([grad_gate, grad_up], axis=1)
    (mixed, gres, dq, kg, vg, gg, nrm_c, cot_c, gres_c, gu_all, act_all, att_all) = call(
        back,
        [
            ((8, 4096), BF),
            ((8, 4096), BF),
            ((128, 256), BF),
            ((8, 1024), F32),
            ((8, 1024), F32),
            ((1, 4096), F32),
            ((8, 16, 8, 512), BF),
            ((8, 16, 8, 512), BF),
            ((8, 16, 8, 512), BF),
            ((8, 128, 896), BF),
            ((8, 128, 448), BF),
            ((8, 128, 256), BF),
        ],
        [((8, 8, 4096), BF)] * 6
        + [
            ((8, 4096), BF),
            ((16, 8, 4096), BF),
            ((128, 256), BF),
            ((8, 128, 256), BF),
            ((8, 128), F32),
            ((8, 8, 128), F32),
            ((16, 8, 256), F32),
            ((16, 8, 256), F32),
            ((1, 4096), F32),
            ((1, 4096), F32),
            ((8, 1, 4096), F32),
            ((1, 4096), F32),
            ((8, 1, 4096), F32),
        ],
        140,
        1,
        (
            gn.reshape(8, 2, 8, 4096), mx.reshape(8, 2, 8, 4096), hid, inv, cotangent, gain,
            nrm_all, cot_all, gu, activated, att, w_out, queries, q_all, k_all, v_all,
            pos_all, doc, lse,
        ),
    )
    nrm_c = nrm_c.reshape(1024, 512)
    cot_c = cot_c.reshape(1024, 512)
    gres_c = gres_c.reshape(1024, 512)
    gu_all = gu_all.reshape(1024, 896)
    contract = functools.partial(
        lax.dot_general,
        dimension_numbers=(((0,), (0,)), ((), ())),
        preferred_element_type=F32,
    )
    grad_w_out = contract(att_all.reshape(1024, 256), gres_c)
    grad_w_gate = contract(nrm_c, gu_all[:, :448])
    grad_w_up = contract(nrm_c, gu_all[:, 448:])
    grad_w_down = contract(act_all.reshape(1024, 448), cot_c)
    return (
        mixed, gres, dq, kg, vg, gg.reshape(4096), grad_w_out, grad_w_gate, grad_w_up, grad_w_down,
    )


def solution(mesh):
    rows = P(("ctx", "ffn"), None)
    return jax.shard_map(
        body,
        mesh=mesh,
        in_specs=(
            rows, P("ctx", "ffn"), P("ctx", None), P("ctx", None), P("ffn", None), P(),
            P(None, "ffn"), P(None, "ffn"), P("ffn", None), rows, P("ctx"), P(),
        ),
        out_specs=(
            rows, rows, P("ctx", "ffn"), rows, rows, P(), P("ffn", "ctx"), P("ctx", "ffn"),
            P("ctx", "ffn"), P("ffn", "ctx"),
        ),
        check_vma=False,
    )
```

```python
import functools
import math

import jax
import jax.numpy as jnp
from jax import lax
from jax.experimental import pallas as pl
from jax.experimental.pallas import tpu as pltpu
from jax.sharding import PartitionSpec as P

MESH = pl.DeviceIdType.MESH
F32 = jnp.float32
BF = jnp.bfloat16
CTX = 8
CHIPS = 8
HW = 128
SCALE = 1.0 / math.sqrt(128)
NEG = -1e30
EPS = 1e-05
NT = (((1,), (1,)), ((), ()))


CHUNKS = 2
WIDE = 4096 // CHUNKS
FAR = [(1, 0), (3, 0), (0, 1), (1, 1), (3, 1), (2, 0), (2, 1)]


class Net:
    def __init__(self, ssem, rsem):
        self.ssem, self.rsem, self.used = ssem, rsem, 0
        self.sent = []
        self.c = lax.axis_index("ctx")
        self.f = lax.axis_index("ffn")
        self.core = lax.rem(self.f, 2)
        self.chip = self.f // 2
        self.partner = self.f + 1 - 2 * self.core

    def copy(self, src, dst, c=None, f=None):
        n = self.used
        self.used = n + 1
        cp = pltpu.make_async_remote_copy(
            src_ref=src,
            dst_ref=dst,
            send_sem=self.ssem.at[n],
            recv_sem=self.rsem.at[n],
            device_id=(self.c if c is None else c, self.f if f is None else f),
            device_id_type=MESH,
        )
        self.sent.append(cp)
        return cp

    def local(self, src, dst):
        n = self.used
        self.used = n + 1
        return pltpu.make_async_copy(src, dst, self.rsem.at[n])

    def done(self, copies):
        for cp in copies:
            cp.wait_send()
            self.sent = [s for s in self.sent if s is not cp]

    def drain(self):
        self.done(list(self.sent))

    def ctx_at(self, d):
        x, y = self.c // 2, lax.rem(self.c, 2)
        return lax.rem(x + d[0], 4) * 2 + lax.rem(y + d[1], 2)

    def ctx_from(self, d):
        return self.ctx_at((4 - d[0], d[1]))

    def chip_at(self, d):
        z, y = self.chip // 2, lax.rem(self.chip, 2)
        return lax.rem(z + d[0], 4) * 2 + lax.rem(y + d[1], 2)

    def chip_from(self, d):
        return self.chip_at((4 - d[0], d[1]))

    def greet(self):
        barrier = pltpu.get_barrier_semaphore()
        for d in FAR:
            pl.semaphore_signal(
                barrier, inc=1, device_id=(self.ctx_at(d), self.f), device_id_type=MESH
            )
        for k in range(1, 16):
            pl.semaphore_signal(
                barrier,
                inc=1,
                device_id=(self.c, lax.rem(self.f + k, 16)),
                device_id_type=MESH,
            )
        pl.semaphore_wait(barrier, 22)


def start_all(copies):
    for cp in copies:
        cp.start()


def wait_all(copies):
    for cp in copies:
        cp.wait_recv()


def ctx_gather(net, src, dst):
    return [net.copy(src, dst.at[net.c], c=net.ctx_at(d)) for d in FAR]


class CtxRelay:
    def __init__(self, net, src, buf):
        self.net, self.buf = net, buf
        mine = buf.at[net.c]
        self.pair = net.copy(src, mine, c=net.ctx_at((0, 1)))
        self.up = net.copy(src, mine, c=net.ctx_at((1, 0)))
        self.down = net.copy(src, mine, c=net.ctx_at((3, 0)))

    def start(self):
        self.pair.start()
        self.up.start()
        self.down.start()

    def pump(self):
        net, buf = self.net, self.buf
        self.pair.wait_recv()
        other = buf.at[net.ctx_at((0, 1))]
        self.up2 = net.copy(other, other, c=net.ctx_at((1, 0)))
        self.down2 = net.copy(other, other, c=net.ctx_at((3, 0)))
        self.up2.start()
        self.down2.start()
        self.up.wait_recv()
        below = buf.at[net.ctx_at((3, 0))]
        self.up3 = net.copy(below, below, c=net.ctx_at((1, 0)))
        self.up3.start()
        self.down2.wait_recv()
        above = buf.at[net.ctx_at((1, 1))]
        self.down3 = net.copy(above, above, c=net.ctx_at((3, 0)))
        self.down3.start()

    def finish(self):
        wait_all([self.down, self.up2, self.up3, self.down3])


class CtxColumns:
    def __init__(self, net, src, dst):
        self.net, self.dst = net, dst
        half = pl.ds(net.core * 8, 8)
        self.half = half
        self.far = []
        for d in FAR:
            to = net.ctx_at(d)
            cols = pl.ds(pl.multiple_of(to * 512, 512), 512)
            self.far.append(net.copy(src.at[half, :, cols], dst.at[net.c, half], c=to))

    def start(self):
        start_all(self.far)

    def forward(self):
        net = self.net
        self.near = []
        for d, cp in zip(FAR, self.far):
            cp.wait_recv()
            block = self.dst.at[net.ctx_from(d), self.half]
            near = net.copy(block, block, f=net.partner)
            near.start()
            self.near.append(near)

    def finish(self):
        wait_all(self.near)


class FfnGather:
    def __init__(self, net, src, dst):
        self.net, self.dst = net, dst
        self.far = [net.copy(src, dst.at[net.f], f=net.chip_at(d) * 2 + net.core) for d in FAR]
        self.near = [net.copy(src, dst.at[net.f], f=net.partner)]

    def start(self):
        start_all(self.far)
        self.near[0].start()

    def forward(self):
        net = self.net
        for d, cp in zip(FAR, self.far):
            cp.wait_recv()
            block = self.dst.at[net.chip_from(d) * 2 + net.core]
            near = net.copy(block, block, f=net.partner)
            near.start()
            self.near.append(near)

    def finish(self):
        wait_all(self.near)


class FfnScatter:
    def __init__(self, net, part, pair_in, summed, got):
        self.net, self.part, self.pair_in, self.summed, self.got = net, part, pair_in, summed, got
        self.pair, self.far = [], []
        for n in range(CHUNKS):
            span = pl.ds(n * WIDE, WIDE)
            self.pair.append(
                net.copy(
                    part.at[:, 1 - net.core, :, span], pair_in.at[:, :, span], f=net.partner
                )
            )
            self.far.append(
                [
                    net.copy(
                        summed.at[net.chip_at(d), :, span],
                        got.at[net.chip, :, span],
                        f=net.chip_at(d) * 2 + net.core,
                    )
                    for d in FAR
                ]
            )

    def put(self, n, product):
        for b in range(16):
            self.part[b // 2, b % 2, :, n * WIDE : (n + 1) * WIDE] = product[
                b * 8 : (b + 1) * 8
            ].astype(BF)
        self.pair[n].start()

    def chip_sum(self, to, n):
        span = slice(n * WIDE, (n + 1) * WIDE)
        return self.part[to, self.net.core, :, span].astype(F32) + self.pair_in[
            to, :, span
        ].astype(F32)

    def middle(self, n):
        net = self.net
        self.pair[n].wait_recv()
        for d, cp in zip(FAR, self.far[n]):
            to = net.chip_at(d)
            self.summed[to, :, n * WIDE : (n + 1) * WIDE] = self.chip_sum(to, n).astype(BF)
            cp.start()

    def finish(self):
        net = self.net
        pieces = []
        for n in range(CHUNKS):
            total = self.chip_sum(net.chip, n)
            for d, cp in zip(FAR, self.far[n]):
                cp.wait_recv()
                total = total + self.got[
                    net.chip_from(d), :, n * WIDE : (n + 1) * WIDE
                ].astype(F32)
            pieces.append(total)
        return jnp.concatenate(pieces, axis=1)

    def drain(self):
        self.net.done(self.pair + [cp for far in self.far for cp in far])


def seg_starts(doc_ref, pos):
    doc = doc_ref[...]
    start = jnp.zeros_like(pos)
    for v in (1, 2, 3):
        edge = jnp.sum((doc < v).astype(F32))
        start = jnp.where(pos >= edge, jnp.maximum(start, edge), start)
    return start


def as_column(row):
    return jnp.transpose(jnp.broadcast_to(row, (128, 128)))


def as_row(column):
    return jnp.transpose(jnp.broadcast_to(column, (128, 128)))[0:1, :]


def layer(
    keys, values, q, pos, doc, resid, gain, cot, wout_h, wgate_h, wup_h, wdown_h,
    mixed, gres, dq, kg, vg, gg, nrm_c, cot_c, gres_c, gate_all, up_all, act_all, att_all,
    wout, wgate, wup, wdown, att, kv_all, q_all, pos_all, nrm_all, cot_all, grows, xr, gact,
    part, pair_in, summed, got, part2, pair_in2, summed2, got2,
    nbuf, gbuf, act, ggate, gup, ga, ga_all, stats, stats_all,
    kv, kv_in, gsum, gpair, gchip, gctx_b, gctx, ssem, rsem,
):
    net = Net(ssem, rsem)
    c, f = net.c, net.f
    cols = pl.ds(pl.multiple_of(net.chip * 128, 128), 128)
    kv_all[0, c] = keys[:, cols]
    kv_all[1, c] = values[:, cols]
    pos_all[c] = pos[...]
    loads = [
        net.local(wout_h, wout),
        net.local(wdown_h, wdown),
        net.local(wgate_h, wgate),
        net.local(wup_h, wup),
    ]
    start_all(loads)
    net.greet()
    mine = kv_all.at[net.core, c]
    kv_far = [net.copy(mine, mine, c=net.ctx_at(d)) for d in FAR]
    pos_far = ctx_gather(net, pos, pos_all)
    start_all(kv_far)
    start_all(pos_far)
    q_all[c] = q[...]
    cot_all[f] = cot[...]
    cot_ag = FfnGather(net, cot, cot_all)
    q_ag = CtxRelay(net, q, q_all)
    kv_near = []
    for d, cp in zip(FAR, kv_far):
        cp.wait_recv()
        block = kv_all.at[net.core, net.ctx_from(d)]
        near = net.copy(block, block, f=net.partner)
        near.start()
        kv_near.append(near)
    cot_ag.start()
    wait_all(pos_far)
    wait_all(kv_near)
    q_ag.start()
    kpos = jnp.concatenate([pos_all[i] for i in range(CTX)], axis=1)
    qpos = as_column(pos[...])[:, 0:1]
    visible = (kpos <= qpos) & (kpos >= seg_starts(doc, qpos))
    k = kv_all[0].reshape(1024, 128)
    v = kv_all[1].reshape(1024, 128)
    lcol = []
    for h in range(2):
        hs = slice(h * 128, (h + 1) * 128)
        s = lax.dot_general(q[:, hs], k, NT, preferred_element_type=F32) * SCALE
        s = jnp.where(visible, s, NEG)
        top = jnp.max(s, axis=1, keepdims=True)
        w = jnp.where(visible, jnp.exp(s - top), 0.0)
        total = jnp.sum(w, axis=1, keepdims=True)
        o = jnp.dot(w.astype(BF), v, preferred_element_type=F32) / total
        att[:, hs] = o.astype(BF)
        lcol.append(top + jnp.log(total))
    a = att[...]
    loads[0].wait()
    rs = FfnScatter(net, part, pair_in, summed, got)
    for n in range(CHUNKS):
        rs.put(n, jnp.dot(a, wout[:, n * WIDE : (n + 1) * WIDE], preferred_element_type=F32))
    att_all[c] = a
    att_ag = CtxRelay(net, att, att_all)
    for n in range(CHUNKS):
        rs.middle(n)
    cot_ag.forward()
    q_ag.pump()
    att_ag.start()
    cot_ag.finish()
    loads[1].wait()
    rows = jnp.concatenate([cot_all[b] for b in range(16)], axis=0)
    gact[...] = lax.dot_general(rows, wdown[...], NT, preferred_element_type=F32)
    own = pl.ds(pl.multiple_of(c * 512, 512), 512)
    cot_c[c] = cot_all[:, :, own]
    cot_cols = CtxColumns(net, cot_all, cot_c)
    projected = rs.finish()
    hidden = (resid[...].astype(F32) + projected).astype(BF)
    hf = hidden.astype(F32)
    ir = lax.rsqrt(jnp.mean(hf * hf, axis=1, keepdims=True) + EPS)
    normed = (hf * ir * gain[...]).astype(BF)
    nbuf[...] = normed
    nrm_all[f] = normed
    ag = FfnGather(net, nbuf, nrm_all)
    ag.start()
    cot_cols.start()
    ag.forward()
    att_ag.pump()
    ag.finish()
    nrm_cols = CtxColumns(net, nrm_all, nrm_c)
    nrm_cols.start()
    nrm_c[c] = nrm_all[:, :, own]
    xr[...] = jnp.concatenate([nrm_all[b] for b in range(16)], axis=0)
    loads[2].wait()
    gate_pre = jnp.dot(xr[...], wgate[...], preferred_element_type=F32)
    loads[3].wait()
    up_proj = jnp.dot(xr[...], wup[...], preferred_element_type=F32)
    sig = jax.nn.sigmoid(gate_pre)
    grad_act = gact[...]
    activated = (gate_pre * sig * up_proj).astype(BF)
    grad_up = (grad_act * gate_pre * sig).astype(BF)
    grad_gate = (grad_act * up_proj * sig * (1.0 + gate_pre * (1.0 - sig))).astype(BF)
    act[...] = activated
    ggate[...] = grad_gate
    gup[...] = grad_up
    rs.drain()
    rs = FfnScatter(net, part, pair_in, summed, got)
    for n in range(CHUNKS):
        span = slice(n * WIDE, (n + 1) * WIDE)
        rs.put(
            n,
            lax.dot_general(ggate[...], wgate[span, :], NT, preferred_element_type=F32)
            + lax.dot_general(gup[...], wup[span, :], NT, preferred_element_type=F32),
        )
    gate_all[c] = ggate[...]
    up_all[c] = gup[...]
    act_all[c] = act[...]
    gate_ag = CtxRelay(net, ggate, gate_all)
    up_ag = CtxRelay(net, gup, up_all)
    act_ag = CtxRelay(net, act, act_all)
    gate_ag.start()
    up_ag.start()
    act_ag.start()
    for n in range(CHUNKS):
        rs.middle(n)
    cot_cols.forward()
    nrm_cols.forward()
    rs2 = FfnScatter(net, part2, pair_in2, summed2, got2)
    for n in range(CHUNKS):
        rs2.put(
            n, jnp.dot(act[...], wdown[:, n * WIDE : (n + 1) * WIDE], preferred_element_type=F32)
        )
    gate_ag.pump()
    gnorm = rs.finish()
    gained = gnorm * gain[...]
    cube = ir * ir * ir
    mean = jnp.mean(gained * hf, axis=1, keepdims=True)
    gr = (cot[...].astype(F32) + ir * gained - hf * cube * mean).astype(BF)
    gres[...] = gr
    gbuf[...] = gr
    grows[f] = gr
    gsum[...] = jnp.sum(gnorm * hf * ir, axis=0, keepdims=True)
    ag = FfnGather(net, gbuf, grows)
    ag.start()
    g1 = net.copy(gsum, gpair, f=net.partner)
    g1.start()
    up_ag.pump()
    g1.wait_recv()
    gchip[net.chip] = gsum[...] + gpair[...]
    g2 = [
        net.copy(gchip.at[net.chip], gchip.at[net.chip], f=net.chip_at(d) * 2 + net.core)
        for d in FAR
    ]
    start_all(g2)
    ag.forward()
    ag.finish()
    for n in range(CHUNKS):
        rs2.middle(n)
    rows = jnp.concatenate([grows[b] for b in range(16)], axis=0)
    gat = lax.dot_general(rows, wout[...], NT, preferred_element_type=F32).astype(BF)
    ga[...] = gat
    ga_all[c] = gat
    prod = gat.astype(F32) * att[...].astype(F32)
    delta = [jnp.sum(prod[:, h * 128 : (h + 1) * 128], axis=1, keepdims=True) for h in range(2)]
    st = jnp.concatenate(
        [as_row(r) for r in lcol + delta] + [jnp.zeros((4, 128), F32)], axis=0
    )
    stats[...] = st
    stats_all[c] = st
    late = ctx_gather(net, ga, ga_all) + ctx_gather(net, stats, stats_all)
    start_all(late)
    gres_cols = CtxColumns(net, grows, gres_c)
    gres_cols.start()
    gres_c[c] = grows[:, :, own]
    act_ag.pump()
    k = kv_all[0].reshape(1024, 128)
    v = kv_all[1].reshape(1024, 128)
    for h in range(2):
        hs = slice(h * 128, (h + 1) * 128)
        s = lax.dot_general(q[:, hs], k, NT, preferred_element_type=F32) * SCALE
        p = jnp.where(visible, jnp.exp(jnp.where(visible, s, NEG) - lcol[h]), 0.0)
        dp = lax.dot_general(ga[:, hs], v, NT, preferred_element_type=F32)
        ds = (p * (dp - delta[h])).astype(BF)
        dq[:, hs] = (jnp.dot(ds, k, preferred_element_type=F32) * SCALE).astype(BF)
    wait_all(g2)
    tot = gchip[0]
    for i in range(1, CHIPS):
        tot = tot + gchip[i]
    gctx_b[...] = tot
    gctx[c] = tot
    g3 = ctx_gather(net, gctx_b, gctx)
    start_all(g3)
    q_ag.finish()
    wait_all(late)
    vis_t = (qpos <= kpos) & (qpos >= seg_starts(doc, kpos))
    k_own = kv_all[0, c]
    v_own = kv_all[1, c]
    dk = jnp.zeros((128, 128), F32)
    dv = jnp.zeros((128, 128), F32)
    for h in range(2):
        hs = slice(h * 128, (h + 1) * 128)
        qa = q_all[:, :, hs].reshape(1024, 128)
        gaa = ga_all[:, :, hs].reshape(1024, 128)
        lrow = jnp.concatenate([stats_all[i, h : h + 1, :] for i in range(CTX)], axis=1)
        drow = jnp.concatenate([stats_all[i, 2 + h : 3 + h, :] for i in range(CTX)], axis=1)
        s = lax.dot_general(k_own, qa, NT, preferred_element_type=F32) * SCALE
        p = jnp.where(vis_t, jnp.exp(jnp.where(vis_t, s, NEG) - lrow), 0.0)
        dp = lax.dot_general(v_own, gaa, NT, preferred_element_type=F32)
        ds = (p * (dp - drow)).astype(BF)
        dk = dk + jnp.dot(ds, qa, preferred_element_type=F32)
        dv = dv + jnp.dot(p.astype(BF), gaa, preferred_element_type=F32)
    dkv = jnp.concatenate([dk * SCALE, dv], axis=1)
    for b in range(16):
        kv[b] = dkv[b * 8 : (b + 1) * 8]
    kv_in[f] = kv[f]
    last = []
    for n in range(1, 16):
        to = lax.rem(f + n, 16)
        last.append(net.copy(kv.at[to], kv_in.at[f], f=to))
    start_all(last)
    gres_cols.forward()
    mixed[...] = (hf + rs2.finish()).astype(BF)
    wait_all(g3)
    tot = gctx[0]
    for i in range(1, CTX):
        tot = tot + gctx[i]
    gg[...] = tot
    wait_all(last)
    for g in range(8):
        pair = kv_in[2 * g] + kv_in[2 * g + 1]
        kg[:, g * 128 : (g + 1) * 128] = pair[:, 0:128]
        vg[:, g * 128 : (g + 1) * 128] = pair[:, 128:256]
    for gather in (cot_cols, nrm_cols, gres_cols, gate_ag, up_ag, act_ag, att_ag):
        gather.finish()
    net.drain()


VM = pl.BlockSpec(memory_space=pltpu.VMEM)
ANY = pl.BlockSpec(memory_space=pl.ANY)
SEMS = 320


def body(
    resid_in, queries, keys_in, value_rows_input, w_out, norm_gain, w_gate, w_up, w_down,
    cotangent, positions, doc_ids,
):
    pos = positions.astype(F32).reshape(1, 128)
    doc = doc_ids.reshape(8, 128)
    gain = norm_gain.reshape(1, 4096)
    outs = [
        ((8, 4096), BF),
        ((8, 4096), BF),
        ((128, 256), BF),
        ((8, 1024), F32),
        ((8, 1024), F32),
        ((1, 4096), F32),
        ((8, 16, 8, 512), BF),
        ((8, 16, 8, 512), BF),
        ((8, 16, 8, 512), BF),
        ((8, 128, 448), BF),
        ((8, 128, 448), BF),
        ((8, 128, 448), BF),
        ((8, 128, 256), BF),
    ]
    scratch = [
        ((256, 4096), BF),
        ((4096, 448), BF),
        ((4096, 448), BF),
        ((448, 4096), BF),
        ((128, 256), BF),
        ((2, 8, 128, 128), BF),
        ((8, 128, 256), BF),
        ((8, 1, 128), F32),
        ((16, 8, 4096), BF),
        ((16, 8, 4096), BF),
        ((16, 8, 4096), BF),
        ((128, 4096), BF),
        ((128, 448), F32),
    ]
    scratch += [((8, 2, 8, 4096), BF)] + [((8, 8, 4096), BF)] * 3
    scratch += [((8, 2, 8, 4096), BF)] + [((8, 8, 4096), BF)] * 3
    scratch += [
        ((8, 4096), BF),
        ((8, 4096), BF),
        ((128, 448), BF),
        ((128, 448), BF),
        ((128, 448), BF),
        ((128, 256), BF),
        ((8, 128, 256), BF),
        ((8, 128), F32),
        ((8, 8, 128), F32),
        ((16, 8, 256), F32),
        ((16, 8, 256), F32),
        ((1, 4096), F32),
        ((1, 4096), F32),
        ((8, 1, 4096), F32),
        ((1, 4096), F32),
        ((8, 1, 4096), F32),
    ]
    (mixed, gres, dq, kg, vg, gg, nrm_c, cot_c, gres_c, gate_all, up_all, act_all, att_all) = (
        pl.pallas_call(
            layer,
            out_shape=[jax.ShapeDtypeStruct(s, d) for s, d in outs],
            in_specs=[VM] * 8 + [ANY] * 4,
            out_specs=[VM] * len(outs),
            scratch_shapes=[pltpu.VMEM(s, d) for s, d in scratch]
            + [pltpu.SemaphoreType.DMA((SEMS,)), pltpu.SemaphoreType.DMA((SEMS,))],
            compiler_params=pltpu.CompilerParams(
                collective_id=0, has_side_effects=True, vmem_limit_bytes=60 * 2**20
            ),
        )(
            keys_in, value_rows_input, queries, pos, doc, resid_in, gain, cotangent,
            w_out, w_gate, w_up, w_down,
        )
    )
    contract = functools.partial(
        lax.dot_general,
        dimension_numbers=(((0,), (0,)), ((), ())),
        preferred_element_type=F32,
    )
    nrm_c = nrm_c.reshape(1024, 512)
    grad_w_out = contract(att_all.reshape(1024, 256), gres_c.reshape(1024, 512))
    grad_w_gate = contract(nrm_c, gate_all.reshape(1024, 448))
    grad_w_up = contract(nrm_c, up_all.reshape(1024, 448))
    grad_w_down = contract(act_all.reshape(1024, 448), cot_c.reshape(1024, 512))
    return (
        mixed, gres, dq, kg, vg, gg.reshape(4096), grad_w_out, grad_w_gate, grad_w_up, grad_w_down,
    )


def solution(mesh):
    rows = P(("ctx", "ffn"), None)
    return jax.shard_map(
        body,
        mesh=mesh,
        in_specs=(
            rows, P("ctx", "ffn"), P("ctx", None), P("ctx", None), P("ffn", None), P(),
            P(None, "ffn"), P(None, "ffn"), P("ffn", None), rows, P("ctx"), P(),
        ),
        out_specs=(
            rows, rows, P("ctx", "ffn"), rows, rows, P(), P("ffn", "ctx"), P("ctx", "ffn"),
            P("ctx", "ffn"), P("ffn", "ctx"),
        ),
        check_vma=False,
    )
```

```python
import functools
import math

import jax
import jax.numpy as jnp
from jax import lax
from jax.experimental import pallas as pl
from jax.experimental.pallas import tpu as pltpu
from jax.sharding import PartitionSpec as P

MESH = pl.DeviceIdType.MESH
F32 = jnp.float32
BF = jnp.bfloat16
CTX = 8
CHIPS = 8
HW = 128
SCALE = 1.0 / math.sqrt(128)
NEG = -1e30
EPS = 1e-05
NT = (((1,), (1,)), ((), ()))


CHUNKS = 2
WIDE = 4096 // CHUNKS
FAR = [(1, 0), (3, 0), (0, 1), (1, 1), (3, 1), (2, 0), (2, 1)]


class Copy:
    def __init__(self, net, cp):
        self.net, self.cp = net, cp

    def start(self):
        self.net.to_send.append(self)
        self.net.to_recv.append(self)
        self.cp.start()

    def wait_recv(self):
        self.net.to_recv = [s for s in self.net.to_recv if s is not self]
        self.cp.wait_recv()

    def wait_send(self):
        self.net.to_send = [s for s in self.net.to_send if s is not self]
        self.cp.wait_send()


class Load(Copy):
    def start(self):
        self.net.to_recv.append(self)
        self.cp.start()

    def wait_recv(self):
        self.net.to_recv = [s for s in self.net.to_recv if s is not self]
        self.cp.wait()


class Net:
    def __init__(self, ssem, rsem):
        self.ssem, self.rsem, self.used = ssem, rsem, 0
        self.to_send, self.to_recv = [], []
        self.c = lax.axis_index("ctx")
        self.f = lax.axis_index("ffn")
        self.core = lax.rem(self.f, 2)
        self.chip = self.f // 2
        self.partner = self.f + 1 - 2 * self.core

    def copy(self, src, dst, c=None, f=None):
        n = self.used
        self.used = n + 1
        cp = pltpu.make_async_remote_copy(
            src_ref=src,
            dst_ref=dst,
            send_sem=self.ssem.at[n],
            recv_sem=self.rsem.at[n],
            device_id=(self.c if c is None else c, self.f if f is None else f),
            device_id_type=MESH,
        )
        return Copy(self, cp)

    def local(self, src, dst):
        n = self.used
        self.used = n + 1
        return Load(self, pltpu.make_async_copy(src, dst, self.rsem.at[n]))

    def drain(self):
        for cp in list(self.to_recv):
            cp.wait_recv()
        for cp in list(self.to_send):
            cp.wait_send()

    def ctx_at(self, d):
        x, y = self.c // 2, lax.rem(self.c, 2)
        return lax.rem(x + d[0], 4) * 2 + lax.rem(y + d[1], 2)

    def ctx_from(self, d):
        return self.ctx_at((4 - d[0], d[1]))

    def chip_at(self, d):
        z, y = self.chip // 2, lax.rem(self.chip, 2)
        return lax.rem(z + d[0], 4) * 2 + lax.rem(y + d[1], 2)

    def chip_from(self, d):
        return self.chip_at((4 - d[0], d[1]))

    def greet(self):
        barrier = pltpu.get_barrier_semaphore()
        for d in FAR:
            pl.semaphore_signal(
                barrier, inc=1, device_id=(self.ctx_at(d), self.f), device_id_type=MESH
            )
        for k in range(1, 16):
            pl.semaphore_signal(
                barrier,
                inc=1,
                device_id=(self.c, lax.rem(self.f + k, 16)),
                device_id_type=MESH,
            )
        pl.semaphore_wait(barrier, 22)


def start_all(copies):
    for cp in copies:
        cp.start()


def wait_all(copies):
    for cp in copies:
        cp.wait_recv()


def ctx_gather(net, src, dst):
    return [net.copy(src, dst.at[net.c], c=net.ctx_at(d)) for d in FAR]


class Relay:
    def __init__(self, net, src, slot, at, send, share):
        self.net, self.slot, self.at, self.send, self.share = net, slot, at, send, share
        self.near = []
        mine = slot(at((0, 0)))
        self.pair = send(src, mine, (0, 1))
        self.up = send(src, mine, (1, 0))
        self.down = send(src, mine, (3, 0))
        if share:
            self.near.append(net.copy(src, mine, f=net.partner))

    def start(self):
        start_all([self.pair, self.up, self.down] + self.near)

    def take(self, cp, d):
        cp.wait_recv()
        block = self.slot(self.at(d))
        if self.share:
            near = self.net.copy(block, block, f=self.net.partner)
            near.start()
            self.near.append(near)
        return block

    def pump(self):
        other = self.take(self.pair, (0, 1))
        self.up2 = self.send(other, other, (1, 0))
        self.down2 = self.send(other, other, (3, 0))
        start_all([self.up2, self.down2])
        below = self.take(self.up, (3, 0))
        self.up3 = self.send(below, below, (1, 0))
        self.up3.start()
        above = self.take(self.down2, (1, 1))
        self.down3 = self.send(above, above, (3, 0))
        self.down3.start()

    def finish(self):
        self.take(self.down, (1, 0))
        self.take(self.up2, (3, 1))
        self.take(self.up3, (2, 0))
        self.take(self.down3, (2, 1))

    def close(self):
        wait_all(self.near)


def ctx_relay(net, src, slot):
    return Relay(
        net, src, slot, net.ctx_at, lambda s, t, d: net.copy(s, t, c=net.ctx_at(d)), False
    )


def ffn_relay(net, src, slot):
    def at(d):
        return net.chip_at(d) * 2 + net.core

    return Relay(net, src, slot, at, lambda s, t, d: net.copy(s, t, f=at(d)), True)


class Columns:
    def __init__(self, net, src, mid, dst):
        self.net, self.mid, self.dst = net, mid, dst
        own = pl.ds(pl.multiple_of(net.c * 512, 512), 512)
        mid[net.c] = src[:, own]
        self.far = []
        for d in FAR:
            to = net.ctx_at(d)
            cols = pl.ds(pl.multiple_of(to * 512, 512), 512)
            self.far.append(net.copy(src.at[:, cols], mid.at[net.c], c=to))

    def start(self):
        start_all(self.far)

    def middle(self):
        wait_all(self.far)
        self.dst[:, self.net.f] = self.mid[...]
        self.relay = ffn_relay(self.net, self.mid, lambda i: self.dst.at[:, i])
        self.relay.start()

    def pump(self):
        self.relay.pump()

    def finish(self):
        self.relay.finish()

    def close(self):
        self.relay.close()


class FfnGather:
    def __init__(self, net, src, dst):
        self.net, self.dst = net, dst
        self.far = [net.copy(src, dst.at[net.f], f=net.chip_at(d) * 2 + net.core) for d in FAR]
        self.near = [net.copy(src, dst.at[net.f], f=net.partner)]

    def start(self):
        start_all(self.far)
        self.near[0].start()

    def forward(self):
        net = self.net
        for d, cp in zip(FAR, self.far):
            cp.wait_recv()
            block = self.dst.at[net.chip_from(d) * 2 + net.core]
            near = net.copy(block, block, f=net.partner)
            near.start()
            self.near.append(near)

    def finish(self):
        wait_all(self.near)


class FfnScatter:
    def __init__(self, net, part, pair_in, summed, got):
        self.net, self.part, self.pair_in, self.summed, self.got = net, part, pair_in, summed, got
        self.pair, self.far = [], []
        for n in range(CHUNKS):
            span = pl.ds(n * WIDE, WIDE)
            self.pair.append(
                net.copy(
                    part.at[:, 1 - net.core, :, span], pair_in.at[:, :, span], f=net.partner
                )
            )
            self.far.append(
                [
                    net.copy(
                        summed.at[net.chip_at(d), :, span],
                        got.at[net.chip, :, span],
                        f=net.chip_at(d) * 2 + net.core,
                    )
                    for d in FAR
                ]
            )

    def put(self, n, product):
        for b in range(16):
            self.part[b // 2, b % 2, :, n * WIDE : (n + 1) * WIDE] = product[
                b * 8 : (b + 1) * 8
            ].astype(BF)
        self.pair[n].start()

    def chip_sum(self, to, n):
        span = slice(n * WIDE, (n + 1) * WIDE)
        return self.part[to, self.net.core, :, span].astype(F32) + self.pair_in[
            to, :, span
        ].astype(F32)

    def middle(self, n):
        net = self.net
        self.pair[n].wait_recv()
        for d, cp in zip(FAR, self.far[n]):
            to = net.chip_at(d)
            self.summed[to, :, n * WIDE : (n + 1) * WIDE] = self.chip_sum(to, n).astype(BF)
            cp.start()

    def finish(self):
        net = self.net
        pieces = []
        for n in range(CHUNKS):
            total = self.chip_sum(net.chip, n)
            for d, cp in zip(FAR, self.far[n]):
                cp.wait_recv()
                total = total + self.got[
                    net.chip_from(d), :, n * WIDE : (n + 1) * WIDE
                ].astype(F32)
            pieces.append(total)
        return jnp.concatenate(pieces, axis=1)

    def drain(self):
        for cp in self.pair + [cp for far in self.far for cp in far]:
            cp.wait_send()


def seg_starts(doc_ref, pos):
    doc = doc_ref[...]
    start = jnp.zeros_like(pos)
    for v in (1, 2, 3):
        edge = jnp.sum((doc < v).astype(F32))
        start = jnp.where(pos >= edge, jnp.maximum(start, edge), start)
    return start


def as_column(row):
    return jnp.transpose(jnp.broadcast_to(row, (128, 128)))


def as_row(column):
    return jnp.transpose(jnp.broadcast_to(column, (128, 128)))[0:1, :]


def in_rows(blocks):
    return jnp.concatenate([blocks[i, b] for i in range(CTX) for b in range(16)], axis=0)


def flat(blocks):
    return jnp.concatenate([blocks[b] for b in range(16)], axis=0)


def layer(
    keys, values, q, pos, doc, resid, gain, cot, wout_h, wgate_h, wup_h, wdown_h,
    mixed, gres, dq, kg, vg, gg, dwout_h, dwgate_h, dwup_h, dwdown_h,
    wout, wgate, wup, wdown, dwout, dwgate, dwup, dwdown, att, kv_all, q_all, pos_all,
    nrm_all, cot_all, grows, xr, gact,
    part, pair_in, summed, got, part2, pair_in2, summed2, got2,
    nbuf, gbuf, act, ggate, gup, act_t, gate_t, up_t, att_t, act_all, gate_all, up_all, att_all,
    cot_mid, nrm_mid, gres_mid, cot_c, nrm_c, gres_c, ga, ga_all, stats, stats_all,
    kv, kv_in, gsum, gpair, gchip, gctx_b, gctx, ssem, rsem,
):
    net = Net(ssem, rsem)
    c, f = net.c, net.f
    cols = pl.ds(pl.multiple_of(net.chip * 128, 128), 128)
    kv_all[0, c] = keys[:, cols]
    kv_all[1, c] = values[:, cols]
    pos_all[c] = pos[...]
    loads = [
        net.local(wout_h, wout),
        net.local(wdown_h, wdown),
        net.local(wgate_h, wgate),
        net.local(wup_h, wup),
    ]
    start_all(loads)
    net.greet()

    def lanes(i):
        return pl.ds(pl.multiple_of(i * 128, 128), 128)

    mine = kv_all.at[net.core, c]
    kv_far = [net.copy(mine, mine, c=net.ctx_at(d)) for d in FAR]
    pos_far = ctx_gather(net, pos, pos_all)
    start_all(kv_far)
    start_all(pos_far)
    cot_cols = Columns(net, cot, cot_mid, cot_c)
    cot_cols.start()
    cot_all[f] = cot[...]
    cot_ag = ffn_relay(net, cot, lambda i: cot_all.at[i])
    cot_ag.start()
    q_all[c] = q[...]
    q_ag = ctx_relay(net, q, lambda i: q_all.at[i])
    kv_near = []
    for d, cp in zip(FAR, kv_far):
        cp.wait_recv()
        block = kv_all.at[net.core, net.ctx_from(d)]
        near = net.copy(block, block, f=net.partner)
        near.start()
        kv_near.append(near)
    cot_ag.pump()
    q_ag.start()
    wait_all(pos_far)
    wait_all(kv_near)
    kpos = jnp.concatenate([pos_all[i] for i in range(CTX)], axis=1).astype(F32)
    qpos = as_column(pos[...].astype(F32))[:, 0:1]
    visible = (kpos <= qpos) & (kpos >= seg_starts(doc, qpos))
    k = kv_all[0].reshape(1024, 128)
    v = kv_all[1].reshape(1024, 128)
    lcol = []
    for h in range(2):
        hs = slice(h * 128, (h + 1) * 128)
        s = lax.dot_general(q[:, hs], k, NT, preferred_element_type=F32) * SCALE
        s = jnp.where(visible, s, NEG)
        top = jnp.max(s, axis=1, keepdims=True)
        w = jnp.where(visible, jnp.exp(s - top), 0.0)
        total = jnp.sum(w, axis=1, keepdims=True)
        o = jnp.dot(w.astype(BF), v, preferred_element_type=F32) / total
        att[:, hs] = o.astype(BF)
        lcol.append(top + jnp.log(total))
    a = att[...]
    loads[0].wait_recv()
    rs = FfnScatter(net, part, pair_in, summed, got)
    for n in range(CHUNKS):
        rs.put(n, jnp.dot(a, wout[:, n * WIDE : (n + 1) * WIDE], preferred_element_type=F32))
    cot_cols.middle()
    for n in range(CHUNKS):
        rs.middle(n)
    at = jnp.transpose(a.astype(F32)).astype(BF)
    att_t[...] = at
    att_all[:, lanes(c)] = at
    att_ag = ctx_relay(net, att_t, lambda i: att_all.at[:, lanes(i)])
    att_ag.start()
    q_ag.pump()
    cot_ag.finish()
    cot_cols.pump()
    cot_ag.close()
    loads[1].wait_recv()
    gact[...] = lax.dot_general(flat(cot_all), wdown[...], NT, preferred_element_type=F32)
    projected = rs.finish()
    hidden = (resid[...].astype(F32) + projected).astype(BF)
    hf = hidden.astype(F32)
    ir = lax.rsqrt(jnp.mean(hf * hf, axis=1, keepdims=True) + EPS)
    normed = (hf * ir * gain[...]).astype(BF)
    nbuf[...] = normed
    nrm_all[f] = normed
    ag = FfnGather(net, nbuf, nrm_all)
    ag.start()
    nrm_cols = Columns(net, nbuf, nrm_mid, nrm_c)
    nrm_cols.start()
    att_ag.pump()
    cot_cols.finish()
    rs.drain()
    ag.forward()
    ag.finish()
    nrm_cols.middle()
    xr[...] = flat(nrm_all)
    loads[2].wait_recv()
    gate_pre = lax.dot_general(xr[...], wgate[...], NT, preferred_element_type=F32)
    loads[3].wait_recv()
    up_proj = lax.dot_general(xr[...], wup[...], NT, preferred_element_type=F32)
    sig = jax.nn.sigmoid(gate_pre)
    grad_act = gact[...]
    activated = (gate_pre * sig * up_proj).astype(BF)
    grad_up = (grad_act * gate_pre * sig).astype(BF)
    grad_gate = (grad_act * up_proj * sig * (1.0 + gate_pre * (1.0 - sig))).astype(BF)
    act[...] = activated
    ggate[...] = grad_gate
    gup[...] = grad_up
    rs = FfnScatter(net, part, pair_in, summed, got)
    for n in range(CHUNKS):
        span = slice(n * WIDE, (n + 1) * WIDE)
        rs.put(
            n,
            jnp.dot(ggate[...], wgate[:, span], preferred_element_type=F32)
            + jnp.dot(gup[...], wup[:, span], preferred_element_type=F32),
        )
    relays = []
    for src, turned, gathered in ((ggate, gate_t, gate_all), (gup, up_t, up_all), (act, act_t, act_all)):
        turn = jnp.transpose(src[...].astype(F32)).astype(BF)
        turned[...] = turn
        gathered[:, lanes(c)] = turn
        relay = ctx_relay(net, turned, lambda i, gathered=gathered: gathered.at[:, lanes(i)])
        relay.start()
        relays.append(relay)
        if len(relays) <= CHUNKS:
            rs.middle(len(relays) - 1)
    gate_ag, up_ag, act_ag = relays
    nrm_cols.pump()
    rs2 = FfnScatter(net, part2, pair_in2, summed2, got2)
    for n in range(CHUNKS):
        rs2.put(
            n, jnp.dot(act[...], wdown[:, n * WIDE : (n + 1) * WIDE], preferred_element_type=F32)
        )
    gate_ag.pump()
    att_ag.finish()
    gnorm = rs.finish()
    gained = gnorm * gain[...]
    cube = ir * ir * ir
    mean = jnp.mean(gained * hf, axis=1, keepdims=True)
    gr = (cot[...].astype(F32) + ir * gained - hf * cube * mean).astype(BF)
    gres[...] = gr
    gbuf[...] = gr
    grows[f] = gr
    gsum[...] = jnp.sum(gnorm * hf * ir, axis=0, keepdims=True)
    ag = FfnGather(net, gbuf, grows)
    ag.start()
    gres_cols = Columns(net, gbuf, gres_mid, gres_c)
    gres_cols.start()
    g1 = net.copy(gsum, gpair, f=net.partner)
    g1.start()
    up_ag.pump()
    nrm_cols.finish()
    g1.wait_recv()
    gchip[net.chip] = gsum[...] + gpair[...]
    g2 = [
        net.copy(gchip.at[net.chip], gchip.at[net.chip], f=net.chip_at(d) * 2 + net.core)
        for d in FAR
    ]
    start_all(g2)
    act_ag.pump()
    ag.forward()
    ag.finish()
    gat = lax.dot_general(flat(grows), wout[...], NT, preferred_element_type=F32).astype(BF)
    ga[...] = gat
    ga_all[c] = gat
    prod = gat.astype(F32) * a.astype(F32)
    delta = [jnp.sum(prod[:, h * 128 : (h + 1) * 128], axis=1, keepdims=True) for h in range(2)]
    st = jnp.concatenate(
        [as_row(r) for r in lcol + delta] + [jnp.zeros((4, 128), F32)], axis=0
    )
    stats[...] = st
    stats_all[c] = st
    late = ctx_gather(net, ga, ga_all) + ctx_gather(net, stats, stats_all)
    start_all(late)
    gres_cols.middle()
    for n in range(CHUNKS):
        rs2.middle(n)
    k = kv_all[0].reshape(1024, 128)
    v = kv_all[1].reshape(1024, 128)
    for h in range(2):
        hs = slice(h * 128, (h + 1) * 128)
        s = lax.dot_general(q[:, hs], k, NT, preferred_element_type=F32) * SCALE
        p = jnp.where(visible, jnp.exp(jnp.where(visible, s, NEG) - lcol[h]), 0.0)
        dp = lax.dot_general(ga[:, hs], v, NT, preferred_element_type=F32)
        ds = (p * (dp - delta[h])).astype(BF)
        dq[:, hs] = (jnp.dot(ds, k, preferred_element_type=F32) * SCALE).astype(BF)
    wait_all(g2)
    tot = gchip[0]
    for i in range(1, CHIPS):
        tot = tot + gchip[i]
    gctx_b[...] = tot
    gctx[c] = tot
    g3 = ctx_gather(net, gctx_b, gctx)
    start_all(g3)
    gres_cols.pump()
    nrm_cols.close()
    gate_ag.finish()
    up_ag.finish()
    rows = in_rows(nrm_c)
    stores = []

    def weight_gradient(left, right, buf, out):
        buf[...] = jnp.dot(left[...], right, preferred_element_type=F32)
        store = net.local(buf, out)
        store.start()
        stores.append(store)

    weight_gradient(gate_all, rows, dwgate, dwgate_h)
    weight_gradient(up_all, rows, dwup, dwup_h)
    q_ag.finish()
    wait_all(late)
    vis_t = (qpos <= kpos) & (qpos >= seg_starts(doc, kpos))
    k_own = kv_all[0, c]
    v_own = kv_all[1, c]
    dk = jnp.zeros((128, 128), F32)
    dv = jnp.zeros((128, 128), F32)
    for h in range(2):
        hs = slice(h * 128, (h + 1) * 128)
        qa = q_all[:, :, hs].reshape(1024, 128)
        gaa = ga_all[:, :, hs].reshape(1024, 128)
        lrow = jnp.concatenate([stats_all[i, h : h + 1, :] for i in range(CTX)], axis=1)
        drow = jnp.concatenate([stats_all[i, 2 + h : 3 + h, :] for i in range(CTX)], axis=1)
        s = lax.dot_general(k_own, qa, NT, preferred_element_type=F32) * SCALE
        p = jnp.where(vis_t, jnp.exp(jnp.where(vis_t, s, NEG) - lrow), 0.0)
        dp = lax.dot_general(v_own, gaa, NT, preferred_element_type=F32)
        ds = (p * (dp - drow)).astype(BF)
        dk = dk + jnp.dot(ds, qa, preferred_element_type=F32)
        dv = dv + jnp.dot(p.astype(BF), gaa, preferred_element_type=F32)
    dkv = jnp.concatenate([dk * SCALE, dv], axis=1)
    for b in range(16):
        kv[b] = dkv[b * 8 : (b + 1) * 8]
    kv_in[f] = kv[f]
    last = []
    for n in range(1, 16):
        to = lax.rem(f + n, 16)
        last.append(net.copy(kv.at[to], kv_in.at[f], f=to))
    start_all(last)
    gres_cols.finish()
    mixed[...] = (hf + rs2.finish()).astype(BF)
    act_ag.finish()
    cot_cols.close()
    weight_gradient(act_all, in_rows(cot_c), dwdown, dwdown_h)
    gres_cols.close()
    weight_gradient(att_all, in_rows(gres_c), dwout, dwout_h)
    wait_all(g3)
    tot = gctx[0]
    for i in range(1, CTX):
        tot = tot + gctx[i]
    gg[...] = tot
    wait_all(last)
    for g in range(8):
        pair = kv_in[2 * g] + kv_in[2 * g + 1]
        kg[:, g * 128 : (g + 1) * 128] = pair[:, 0:128]
        vg[:, g * 128 : (g + 1) * 128] = pair[:, 128:256]
    wait_all(stores)
    net.drain()


def hand_over(*refs):
    n = (len(refs) - 1) // 2
    sems = refs[-1]
    copies = [
        pltpu.make_async_copy(refs[i], refs[n + i], sems.at[i]) for i in range(n)
    ]
    for cp in copies:
        cp.start()
    for cp in copies:
        cp.wait()


VM = pl.BlockSpec(memory_space=pltpu.VMEM)
ANY = pl.BlockSpec(memory_space=pl.ANY)
SEMS = 320


def body(
    resid_in, queries, keys_in, value_rows_input, w_out, norm_gain, w_gate, w_up, w_down,
    cotangent, positions, doc_ids,
):
    small = [
        ((8, 4096), BF),
        ((8, 4096), BF),
        ((128, 256), BF),
        ((8, 1024), F32),
        ((8, 1024), F32),
        ((1, 4096), F32),
    ]
    grads = [((256, 512), F32)] + [((448, 512), F32)] * 3
    shard = [((8, 2, 8, 4096), BF)] + [((8, 8, 4096), BF)] * 3
    scratch = (
        [((256, 4096), BF)]
        + [((448, 4096), BF)] * 3
        + grads
        + [
            ((128, 256), BF),
            ((2, 8, 128, 128), BF),
            ((8, 128, 256), BF),
            ((8, 1, 128), jnp.int32),
            ((16, 8, 4096), BF),
            ((16, 8, 4096), BF),
            ((16, 8, 4096), BF),
            ((128, 4096), BF),
            ((128, 448), F32),
        ]
        + shard
        + shard
        + [((8, 4096), BF)] * 2
        + [((128, 448), BF)] * 3
        + [((448, 128), BF)] * 3
        + [((256, 128), BF)]
        + [((448, 1024), BF)] * 3
        + [((256, 1024), BF)]
        + [((8, 8, 512), BF)] * 3
        + [((8, 16, 8, 512), BF)] * 3
        + [
            ((128, 256), BF),
            ((8, 128, 256), BF),
            ((8, 128), F32),
            ((8, 8, 128), F32),
            ((16, 8, 256), F32),
            ((16, 8, 256), F32),
            ((1, 4096), F32),
            ((1, 4096), F32),
            ((8, 1, 4096), F32),
            ((1, 4096), F32),
            ((8, 1, 4096), F32),
        ]
    )
    shapes = [jax.ShapeDtypeStruct(s, d) for s, d in small + grads]
    results = pl.pallas_call(
        layer,
        out_shape=shapes,
        in_specs=[VM] * 8 + [ANY] * 4,
        out_specs=[VM] * len(small) + [ANY] * len(grads),
        scratch_shapes=[pltpu.VMEM(s, d) for s, d in scratch]
        + [pltpu.SemaphoreType.DMA((SEMS,)), pltpu.SemaphoreType.DMA((SEMS,))],
        compiler_params=pltpu.CompilerParams(
            collective_id=0, has_side_effects=True, vmem_limit_bytes=60 * 2**20
        ),
    )(
        keys_in, value_rows_input, queries, positions.reshape(1, 128), doc_ids.reshape(8, 128),
        resid_in, norm_gain.reshape(1, 4096), cotangent, w_out, w_gate.T, w_up.T, w_down,
    )
    mixed, gres, dq, kg, vg, gg, dwout, dwgate, dwup, dwdown = pl.pallas_call(
        hand_over,
        out_shape=shapes,
        in_specs=[VM] * len(shapes),
        out_specs=[ANY] * len(shapes),
        scratch_shapes=[pltpu.SemaphoreType.DMA((len(shapes),))],
    )(*results)
    return (mixed, gres, dq, kg, vg, gg.reshape(4096), dwout, dwgate.T, dwup.T, dwdown)


def solution(mesh):
    rows = P(("ctx", "ffn"), None)
    return jax.shard_map(
        body,
        mesh=mesh,
        in_specs=(
            rows, P("ctx", "ffn"), P("ctx", None), P("ctx", None), P("ffn", None), P(),
            P(None, "ffn"), P(None, "ffn"), P("ffn", None), rows, P("ctx"), P(),
        ),
        out_specs=(
            rows, rows, P("ctx", "ffn"), rows, rows, P(), P("ffn", "ctx"), P("ctx", "ffn"),
            P("ctx", "ffn"), P("ffn", "ctx"),
        ),
        check_vma=False,
    )
```

```python
import functools
import math

import jax
import jax.numpy as jnp
from jax import lax
from jax.experimental import pallas as pl
from jax.experimental.pallas import tpu as pltpu
from jax.sharding import PartitionSpec as P

MESH = pl.DeviceIdType.MESH
F32 = jnp.float32
BF = jnp.bfloat16
CTX = 8
CHIPS = 8
HW = 128
SCALE = 1.0 / math.sqrt(128)
NEG = -1e30
EPS = 1e-05
NT = (((1,), (1,)), ((), ()))


CHUNKS = 2
WIDE = 4096 // CHUNKS
FAR = [(2, 1), (2, 0), (1, 1), (3, 1), (0, 1), (1, 0), (3, 0)]


class Copy:
    def __init__(self, net, cp):
        self.net, self.cp = net, cp

    def start(self):
        self.net.to_send.append(self)
        self.net.to_recv.append(self)
        self.cp.start()

    def wait_recv(self):
        self.net.to_recv = [s for s in self.net.to_recv if s is not self]
        self.cp.wait_recv()

    def wait_send(self):
        self.net.to_send = [s for s in self.net.to_send if s is not self]
        self.cp.wait_send()


class Load(Copy):
    def start(self):
        self.net.to_recv.append(self)
        self.cp.start()

    def wait_recv(self):
        self.net.to_recv = [s for s in self.net.to_recv if s is not self]
        self.cp.wait()


class Net:
    def __init__(self, ssem, rsem):
        self.ssem, self.rsem, self.used = ssem, rsem, 0
        self.to_send, self.to_recv = [], []
        self.c = lax.axis_index("ctx")
        self.f = lax.axis_index("ffn")
        self.core = lax.rem(self.f, 2)
        self.chip = self.f // 2
        self.partner = self.f + 1 - 2 * self.core

    def copy(self, src, dst, c=None, f=None):
        n = self.used
        self.used = n + 1
        cp = pltpu.make_async_remote_copy(
            src_ref=src,
            dst_ref=dst,
            send_sem=self.ssem.at[n],
            recv_sem=self.rsem.at[n],
            device_id=(self.c if c is None else c, self.f if f is None else f),
            device_id_type=MESH,
        )
        return Copy(self, cp)

    def local(self, src, dst):
        n = self.used
        self.used = n + 1
        return Load(self, pltpu.make_async_copy(src, dst, self.rsem.at[n]))

    def drain(self):
        for cp in list(self.to_recv):
            cp.wait_recv()
        for cp in list(self.to_send):
            cp.wait_send()

    def ctx_at(self, d):
        x, y = self.c // 2, lax.rem(self.c, 2)
        return lax.rem(x + d[0], 4) * 2 + lax.rem(y + d[1], 2)

    def ctx_from(self, d):
        return self.ctx_at((4 - d[0], d[1]))

    def chip_at(self, d):
        z, y = self.chip // 2, lax.rem(self.chip, 2)
        return lax.rem(z + d[0], 4) * 2 + lax.rem(y + d[1], 2)

    def chip_from(self, d):
        return self.chip_at((4 - d[0], d[1]))

    def greet(self):
        barrier = pltpu.get_barrier_semaphore()
        for d in FAR:
            pl.semaphore_signal(
                barrier, inc=1, device_id=(self.ctx_at(d), self.f), device_id_type=MESH
            )
        for k in range(1, 16):
            pl.semaphore_signal(
                barrier,
                inc=1,
                device_id=(self.c, lax.rem(self.f + k, 16)),
                device_id_type=MESH,
            )
        self.barrier = barrier

    def met(self):
        pl.semaphore_wait(self.barrier, 22)


def start_all(copies):
    for cp in copies:
        cp.start()


def wait_all(copies):
    for cp in copies:
        cp.wait_recv()


def ctx_gather(net, src, dst):
    return [net.copy(src, dst.at[net.c], c=net.ctx_at(d)) for d in FAR]


class Relay:
    def __init__(self, net, src, slot, at, send, share):
        self.net, self.slot, self.at, self.send, self.share = net, slot, at, send, share
        self.near = []
        mine = slot(at((0, 0)))
        self.pair = send(src, mine, (0, 1))
        self.up = send(src, mine, (1, 0))
        self.down = send(src, mine, (3, 0))
        if share:
            self.near.append(net.copy(src, mine, f=net.partner))

    def start(self):
        self.start_pair()
        self.start_ring()

    def start_pair(self):
        start_all([self.pair] + self.near)

    def start_ring(self):
        start_all([self.up, self.down])

    def take(self, cp, d):
        cp.wait_recv()
        block = self.slot(self.at(d))
        if self.share:
            near = self.net.copy(block, block, f=self.net.partner)
            near.start()
            self.near.append(near)
        return block

    def pump(self):
        other = self.take(self.pair, (0, 1))
        self.up2 = self.send(other, other, (1, 0))
        self.down2 = self.send(other, other, (3, 0))
        start_all([self.up2, self.down2])
        below = self.take(self.up, (3, 0))
        self.up3 = self.send(below, below, (1, 0))
        self.up3.start()

    def pump2(self):
        above = self.take(self.down2, (1, 1))
        self.down3 = self.send(above, above, (3, 0))
        self.down3.start()

    def finish(self):
        self.take(self.down, (1, 0))
        self.take(self.up2, (3, 1))
        self.take(self.up3, (2, 0))
        self.take(self.down3, (2, 1))

    def close(self):
        wait_all(self.near)


def ctx_relay(net, src, slot):
    return Relay(
        net, src, slot, net.ctx_at, lambda s, t, d: net.copy(s, t, c=net.ctx_at(d)), False
    )


def ffn_relay(net, src, slot):
    def at(d):
        return net.chip_at(d) * 2 + net.core

    return Relay(net, src, slot, at, lambda s, t, d: net.copy(s, t, f=at(d)), True)


class Columns:
    def __init__(self, net, src, mid, dst):
        self.net, self.mid, self.dst = net, mid, dst
        own = pl.ds(pl.multiple_of(net.c * 512, 512), 512)
        mid[net.c] = src[:, own]
        self.far = []
        for d in FAR:
            to = net.ctx_at(d)
            cols = pl.ds(pl.multiple_of(to * 512, 512), 512)
            self.far.append(net.copy(src.at[:, cols], mid.at[net.c], c=to))

    def start(self):
        start_all(self.far)

    def direct(self):
        wait_all(self.far)
        self.dst[:, self.net.f] = self.mid[...]
        self.gather = FfnGather(self.net, self.mid, lambda i: self.dst.at[:, i])
        self.gather.start()

    def middle(self):
        wait_all(self.far)
        self.dst[:, self.net.f] = self.mid[...]
        self.relay = ffn_relay(self.net, self.mid, lambda i: self.dst.at[:, i])
        self.relay.start()

    def pump(self):
        self.relay.pump()

    def pump2(self):
        self.relay.pump2()

    def finish(self):
        self.relay.finish()

    def close(self):
        self.relay.close()


class FfnGather:
    def __init__(self, net, src, slot):
        self.net, self.slot = net, slot
        mine = slot(net.f)
        self.far = [net.copy(src, mine, f=net.chip_at(d) * 2 + net.core) for d in FAR]
        self.near = [net.copy(src, mine, f=net.partner)]

    def start(self):
        start_all(self.far)
        self.near[0].start()

    def forward(self):
        net = self.net
        for d, cp in zip(FAR, self.far):
            cp.wait_recv()
            block = self.slot(net.chip_from(d) * 2 + net.core)
            near = net.copy(block, block, f=net.partner)
            near.start()
            self.near.append(near)

    def finish(self):
        wait_all(self.near)


class FfnScatter:
    def __init__(self, net, part, pair_in, summed, got):
        self.net, self.part, self.pair_in, self.summed, self.got = net, part, pair_in, summed, got
        self.pair, self.far = [], []
        for n in range(CHUNKS):
            span = pl.ds(n * WIDE, WIDE)
            self.pair.append(
                net.copy(
                    part.at[:, 1 - net.core, :, span], pair_in.at[:, :, span], f=net.partner
                )
            )
            self.far.append(
                [
                    net.copy(
                        summed.at[net.chip_at(d), :, span],
                        got.at[net.chip, :, span],
                        f=net.chip_at(d) * 2 + net.core,
                    )
                    for d in FAR
                ]
            )

    def put(self, n, product):
        for b in range(16):
            self.part[b // 2, b % 2, :, n * WIDE : (n + 1) * WIDE] = product[
                b * 8 : (b + 1) * 8
            ].astype(BF)
        self.pair[n].start()

    def chip_sum(self, to, n):
        span = slice(n * WIDE, (n + 1) * WIDE)
        return self.part[to, self.net.core, :, span].astype(F32) + self.pair_in[
            to, :, span
        ].astype(F32)

    def middle(self, n):
        net = self.net
        self.pair[n].wait_recv()
        for d, cp in zip(FAR, self.far[n]):
            to = net.chip_at(d)
            self.summed[to, :, n * WIDE : (n + 1) * WIDE] = self.chip_sum(to, n).astype(BF)
            cp.start()

    def finish(self):
        net = self.net
        pieces = []
        for n in range(CHUNKS):
            total = self.chip_sum(net.chip, n)
            for d, cp in zip(FAR, self.far[n]):
                cp.wait_recv()
                total = total + self.got[
                    net.chip_from(d), :, n * WIDE : (n + 1) * WIDE
                ].astype(F32)
            pieces.append(total)
        return jnp.concatenate(pieces, axis=1)

    def drain(self):
        for cp in self.pair + [cp for far in self.far for cp in far]:
            cp.wait_send()


class RingScatter(FfnScatter):
    def __init__(self, net, part, pair_in, summed, ring_in, half, half_in):
        self.net, self.part, self.pair_in, self.summed = net, part, pair_in, summed
        self.ring_in, self.half, self.half_in = ring_in, half, half_in
        self.pair = [
            net.copy(
                part.at[:, 1 - net.core, :, pl.ds(n * WIDE, WIDE)],
                pair_in.at[:, :, pl.ds(n * WIDE, WIDE)],
                f=net.partner,
            )
            for n in range(CHUNKS)
        ]

    def middle(self):
        net = self.net
        wait_all(self.pair)
        for chip in range(CHIPS):
            self.summed[chip] = (
                self.part[chip, net.core].astype(F32) + self.pair_in[chip].astype(F32)
            ).astype(BF)
        self.ring = []
        for step in (1, 3, 2):
            to = net.chip_at((step, 0))
            block = self.summed.at[pl.ds(to // 2 * 2, 2)]
            cp = net.copy(block, self.ring_in.at[net.chip // 2], f=to * 2 + net.core)
            cp.start()
            self.ring.append(cp)

    def middle2(self):
        net = self.net
        wait_all(self.ring)
        z, y = net.chip // 2, lax.rem(net.chip, 2)

        def ring_sum(yh):
            total = self.summed[z * 2 + yh].astype(F32)
            for step in (1, 3, 2):
                total = total + self.ring_in[lax.rem(z + step, 4), yh].astype(F32)
            return total

        self.half[...] = ring_sum(1 - y).astype(BF)
        self.across = net.copy(self.half, self.half_in, f=net.chip_at((0, 1)) * 2 + net.core)
        self.across.start()
        self.own = ring_sum(y)

    def finish(self):
        self.across.wait_recv()
        return self.own + self.half_in[...].astype(F32)


def seg_starts(doc_ref, pos):
    doc = doc_ref[...]
    start = jnp.zeros_like(pos)
    for v in (1, 2, 3):
        edge = jnp.sum((doc < v).astype(F32))
        start = jnp.where(pos >= edge, jnp.maximum(start, edge), start)
    return start


def as_column(row):
    return jnp.transpose(jnp.broadcast_to(row, (128, 128)))


def as_row(column):
    return jnp.transpose(jnp.broadcast_to(column, (128, 128)))[0:1, :]


def in_rows(blocks):
    return jnp.concatenate([blocks[i, b] for i in range(CTX) for b in range(16)], axis=0)


def flat(blocks):
    return jnp.concatenate([blocks[b] for b in range(16)], axis=0)


def layer(
    keys_h, values_h, q_h, pos_h, doc_h, resid_h, gain_h, cot_h, wout_h, wgate_h, wup_h, wdown_h,
    mixed_h, gres_h, dq_h, kg_h, vg_h, gg_h, dwout_h, dwgate_h, dwup_h, dwdown_h,
    q, pos, doc, resid, gain, cot, mixed, gres, dq, kg, vg, gg,
    wout, wgate, wup, wdown, dwout, dwgate, dwup, dwdown, att, kv_all, q_all, pos_all,
    nrm_all, cot_all, grows, xr, gact,
    part, pair_in, summed, got, part2, pair_in2, summed2, ring_in, half, half_in,
    nbuf, gbuf, act, ggate, gup, act_t, gate_t, up_t, att_t, act_all, gate_all, up_all, att_all,
    cot_mid, nrm_mid, gres_mid, cot_c, nrm_c, gres_c, ga, ga_all, stats, stats_all,
    kv, kv_in, gsum, gpair, gchip, gctx_b, gctx, ssem, rsem,
):
    net = Net(ssem, rsem)
    c, f = net.c, net.f
    cols = pl.ds(pl.multiple_of(net.chip * 128, 128), 128)
    net.greet()
    stores = []

    def put_out(buf, out):
        store = net.local(buf, out)
        store.start()
        stores.append(store)

    first = [
        net.local(keys_h.at[:, cols], kv_all.at[0, c]),
        net.local(values_h.at[:, cols], kv_all.at[1, c]),
        net.local(pos_h, pos),
        net.local(cot_h, cot),
        net.local(q_h, q),
        net.local(doc_h, doc),
        net.local(resid_h, resid),
        net.local(gain_h, gain),
    ]
    start_all(first)
    loads = [
        net.local(wout_h, wout),
        net.local(wdown_h, wdown),
        net.local(wgate_h, wgate),
        net.local(wup_h, wup),
    ]
    start_all(loads)
    wait_all(first)
    pos_all[c] = pos[...]
    net.met()

    def lanes(i):
        return pl.ds(pl.multiple_of(i * 128, 128), 128)

    mine = kv_all.at[net.core, c]
    kv_far = [net.copy(mine, mine, c=net.ctx_at(d)) for d in FAR]
    pos_far = ctx_gather(net, pos, pos_all)
    start_all(kv_far)
    start_all(pos_far)
    cot_cols = Columns(net, cot, cot_mid, cot_c)
    cot_cols.start()
    cot_all[f] = cot[...]
    cot_ag = ffn_relay(net, cot, lambda i: cot_all.at[i])
    cot_ag.start()
    q_all[c] = q[...]
    q_ag = ctx_relay(net, q, lambda i: q_all.at[i])
    kv_near = []
    for d, cp in zip(FAR, kv_far):
        cp.wait_recv()
        block = kv_all.at[net.core, net.ctx_from(d)]
        near = net.copy(block, block, f=net.partner)
        near.start()
        kv_near.append(near)
    cot_ag.pump()
    wait_all(pos_far)
    wait_all(kv_near)
    kpos = jnp.concatenate([pos_all[i] for i in range(CTX)], axis=1).astype(F32)
    qpos = as_column(pos[...].astype(F32))[:, 0:1]
    visible = (kpos <= qpos) & (kpos >= seg_starts(doc, qpos))
    k = kv_all[0].reshape(1024, 128)
    v = kv_all[1].reshape(1024, 128)
    lcol = []
    for h in range(2):
        hs = slice(h * 128, (h + 1) * 128)
        s = lax.dot_general(q[:, hs], k, NT, preferred_element_type=F32) * SCALE
        s = jnp.where(visible, s, NEG)
        top = jnp.max(s, axis=1, keepdims=True)
        w = jnp.where(visible, jnp.exp(s - top), 0.0)
        total = jnp.sum(w, axis=1, keepdims=True)
        o = jnp.dot(w.astype(BF), v, preferred_element_type=F32) / total
        att[:, hs] = o.astype(BF)
        lcol.append(top + jnp.log(total))
    cot_ag.pump2()
    q_ag.start()
    a = att[...]
    loads[0].wait_recv()
    rs = FfnScatter(net, part, pair_in, summed, got)
    for n in range(CHUNKS):
        rs.put(n, jnp.dot(a, wout[:, n * WIDE : (n + 1) * WIDE], preferred_element_type=F32))
    for n in range(CHUNKS):
        rs.middle(n)
    cot_cols.middle()
    at = jnp.transpose(a.astype(F32)).astype(BF)
    att_t[...] = at
    att_all[:, lanes(c)] = at
    att_ag = ctx_relay(net, att_t, lambda i: att_all.at[:, lanes(i)])
    att_ag.start()
    cot_ag.finish()
    cot_ag.close()
    loads[1].wait_recv()
    gact[...] = lax.dot_general(flat(cot_all), wdown[...], NT, preferred_element_type=F32)
    projected = rs.finish()
    hidden = (resid[...].astype(F32) + projected).astype(BF)
    hf = hidden.astype(F32)
    ir = lax.rsqrt(jnp.mean(hf * hf, axis=1, keepdims=True) + EPS)
    normed = (hf * ir * gain[...]).astype(BF)
    nbuf[...] = normed
    nrm_all[f] = normed
    ag = FfnGather(net, nbuf, lambda i: nrm_all.at[i])
    ag.start()
    nrm_cols = Columns(net, nbuf, nrm_mid, nrm_c)
    nrm_cols.start()
    q_ag.pump()
    cot_cols.pump()
    att_ag.pump()
    rs.drain()
    ag.forward()
    ag.finish()
    q_ag.pump2()
    cot_cols.pump2()
    att_ag.pump2()
    nrm_cols.middle()
    xr[...] = flat(nrm_all)
    loads[2].wait_recv()
    gate_pre = lax.dot_general(xr[...], wgate[...], NT, preferred_element_type=F32)
    loads[3].wait_recv()
    up_proj = lax.dot_general(xr[...], wup[...], NT, preferred_element_type=F32)
    sig = jax.nn.sigmoid(gate_pre)
    grad_act = gact[...]
    activated = (gate_pre * sig * up_proj).astype(BF)
    grad_up = (grad_act * gate_pre * sig).astype(BF)
    grad_gate = (grad_act * up_proj * sig * (1.0 + gate_pre * (1.0 - sig))).astype(BF)
    act[...] = activated
    ggate[...] = grad_gate
    gup[...] = grad_up
    def turned_relay(src, turned, gathered):
        turn = jnp.transpose(src[...].astype(F32)).astype(BF)
        turned[...] = turn
        gathered[:, lanes(c)] = turn
        return ctx_relay(net, turned, lambda i: gathered.at[:, lanes(i)])

    act_ag = turned_relay(act, act_t, act_all)
    act_ag.start()
    gate_ag = turned_relay(ggate, gate_t, gate_all)
    gate_ag.start()
    rs = FfnScatter(net, part, pair_in, summed, got)
    for n in range(CHUNKS):
        span = slice(n * WIDE, (n + 1) * WIDE)
        rs.put(
            n,
            jnp.dot(ggate[...], wgate[:, span], preferred_element_type=F32)
            + jnp.dot(gup[...], wup[:, span], preferred_element_type=F32),
        )
    up_ag = turned_relay(gup, up_t, up_all)
    up_ag.start_ring()
    for n in range(CHUNKS):
        rs.middle(n)
    nrm_cols.pump()
    rs2 = RingScatter(net, part2, pair_in2, summed2, ring_in, half, half_in)
    for n in range(CHUNKS):
        rs2.put(
            n, jnp.dot(act[...], wdown[:, n * WIDE : (n + 1) * WIDE], preferred_element_type=F32)
        )
    cot_cols.finish()
    att_ag.finish()
    q_ag.finish()
    gnorm = rs.finish()
    gained = gnorm * gain[...]
    cube = ir * ir * ir
    mean = jnp.mean(gained * hf, axis=1, keepdims=True)
    gr = (cot[...].astype(F32) + ir * gained - hf * cube * mean).astype(BF)
    gres[...] = gr
    put_out(gres, gres_h)
    gbuf[...] = gr
    grows[f] = gr
    gsum[...] = jnp.sum(gnorm * hf * ir, axis=0, keepdims=True)
    ag = FfnGather(net, gbuf, lambda i: grows.at[i])
    ag.start()
    gres_cols = Columns(net, gbuf, gres_mid, gres_c)
    gres_cols.start()
    g1 = net.copy(gsum, gpair, f=net.partner)
    g1.start()
    up_ag.start_pair()
    rs2.middle()
    g1.wait_recv()
    gchip[net.chip] = gsum[...] + gpair[...]
    g2 = [
        net.copy(gchip.at[net.chip], gchip.at[net.chip], f=net.chip_at(d) * 2 + net.core)
        for d in FAR
    ]
    start_all(g2)
    act_ag.pump()
    gate_ag.pump()
    nrm_cols.pump2()
    ag.forward()
    ag.finish()
    gat = lax.dot_general(flat(grows), wout[...], NT, preferred_element_type=F32).astype(BF)
    ga[...] = gat
    ga_all[c] = gat
    prod = gat.astype(F32) * a.astype(F32)
    delta = [jnp.sum(prod[:, h * 128 : (h + 1) * 128], axis=1, keepdims=True) for h in range(2)]
    st = jnp.concatenate(
        [as_row(r) for r in lcol + delta] + [jnp.zeros((4, 128), F32)], axis=0
    )
    stats[...] = st
    stats_all[c] = st
    late = ctx_gather(net, ga, ga_all) + ctx_gather(net, stats, stats_all)
    start_all(late)
    up_ag.pump()
    act_ag.pump2()
    gate_ag.pump2()
    rs2.middle2()
    gres_cols.direct()
    up_ag.pump2()
    k = kv_all[0].reshape(1024, 128)
    v = kv_all[1].reshape(1024, 128)
    for h in range(2):
        hs = slice(h * 128, (h + 1) * 128)
        s = lax.dot_general(q[:, hs], k, NT, preferred_element_type=F32) * SCALE
        p = jnp.where(visible, jnp.exp(jnp.where(visible, s, NEG) - lcol[h]), 0.0)
        dp = lax.dot_general(ga[:, hs], v, NT, preferred_element_type=F32)
        ds = (p * (dp - delta[h])).astype(BF)
        dq[:, hs] = (jnp.dot(ds, k, preferred_element_type=F32) * SCALE).astype(BF)
    put_out(dq, dq_h)
    wait_all(g2)
    tot = gchip[0]
    for i in range(1, CHIPS):
        tot = tot + gchip[i]
    gctx_b[...] = tot
    gctx[c] = tot
    g3 = ctx_gather(net, gctx_b, gctx)
    start_all(g3)

    def weight_gradient(left, right, buf, out):
        buf[...] = jnp.dot(left[...], right, preferred_element_type=F32)
        put_out(buf, out)

    cot_cols.close()
    act_ag.finish()
    weight_gradient(act_all, in_rows(cot_c), dwdown, dwdown_h)
    wait_all(late)
    vis_t = (qpos <= kpos) & (qpos >= seg_starts(doc, kpos))
    k_own = kv_all[0, c]
    v_own = kv_all[1, c]
    dk = jnp.zeros((128, 128), F32)
    dv = jnp.zeros((128, 128), F32)
    for h in range(2):
        hs = slice(h * 128, (h + 1) * 128)
        qa = q_all[:, :, hs].reshape(1024, 128)
        gaa = ga_all[:, :, hs].reshape(1024, 128)
        lrow = jnp.concatenate([stats_all[i, h : h + 1, :] for i in range(CTX)], axis=1)
        drow = jnp.concatenate([stats_all[i, 2 + h : 3 + h, :] for i in range(CTX)], axis=1)
        s = lax.dot_general(k_own, qa, NT, preferred_element_type=F32) * SCALE
        p = jnp.where(vis_t, jnp.exp(jnp.where(vis_t, s, NEG) - lrow), 0.0)
        dp = lax.dot_general(v_own, gaa, NT, preferred_element_type=F32)
        ds = (p * (dp - drow)).astype(BF)
        dk = dk + jnp.dot(ds, qa, preferred_element_type=F32)
        dv = dv + jnp.dot(p.astype(BF), gaa, preferred_element_type=F32)
    dkv = jnp.concatenate([dk * SCALE, dv], axis=1)
    for b in range(16):
        kv[b] = dkv[b * 8 : (b + 1) * 8]
    kv_in[f] = kv[f]
    last = []
    for n in range(1, 16):
        to = lax.rem(f + n, 16)
        last.append(net.copy(kv.at[to], kv_in.at[f], f=to))
    start_all(last)
    gres_cols.gather.forward()
    mixed[...] = (hf + rs2.finish()).astype(BF)
    put_out(mixed, mixed_h)
    gres_cols.gather.finish()
    nrm_cols.finish()
    gate_ag.finish()
    nrm_cols.close()
    rows = in_rows(nrm_c)
    weight_gradient(gate_all, rows, dwgate, dwgate_h)
    up_ag.finish()
    weight_gradient(up_all, rows, dwup, dwup_h)
    weight_gradient(att_all, in_rows(gres_c), dwout, dwout_h)
    wait_all(g3)
    tot = gctx[0]
    for i in range(1, CTX):
        tot = tot + gctx[i]
    gg[...] = tot
    put_out(gg, gg_h)
    wait_all(last)
    for g in range(8):
        pair = kv_in[2 * g] + kv_in[2 * g + 1]
        kg[:, g * 128 : (g + 1) * 128] = pair[:, 0:128]
        vg[:, g * 128 : (g + 1) * 128] = pair[:, 128:256]
    put_out(kg, kg_h)
    put_out(vg, vg_h)
    wait_all(stores)
    net.drain()


def hand_over(*refs):
    n = (len(refs) - 2) // 3
    held, came, left = refs[2 * n : 3 * n], refs[-2], refs[-1]
    ins = [pltpu.make_async_copy(refs[i], held[i], came.at[i]) for i in range(n)]
    outs = [pltpu.make_async_copy(held[i], refs[n + i], left.at[i]) for i in range(n)]
    for cp in ins:
        cp.start()
    for cp, out in zip(ins, outs):
        cp.wait()
        out.start()
    for out in outs:
        out.wait()


ANY = pl.BlockSpec(memory_space=pl.ANY)
SEMS = 320


def body(
    resid_in, queries, keys_in, value_rows_input, w_out, norm_gain, w_gate, w_up, w_down,
    cotangent, positions, doc_ids,
):
    small = [
        ((8, 4096), BF),
        ((8, 4096), BF),
        ((128, 256), BF),
        ((8, 1024), F32),
        ((8, 1024), F32),
        ((1, 4096), F32),
    ]
    grads = [((256, 512), F32)] + [((448, 512), F32)] * 3
    shard = [((8, 2, 8, 4096), BF)] + [((8, 8, 4096), BF)] * 3
    scratch = (
        [((128, 256), BF), ((1, 128), jnp.int32), ((8, 128), jnp.int32)]
        + [((8, 4096), BF), ((1, 4096), F32), ((8, 4096), BF)]
        + small
        + [((256, 4096), BF)]
        + [((448, 4096), BF)] * 3
        + grads
        + [
            ((128, 256), BF),
            ((2, 8, 128, 128), BF),
            ((8, 128, 256), BF),
            ((8, 1, 128), jnp.int32),
            ((16, 8, 4096), BF),
            ((16, 8, 4096), BF),
            ((16, 8, 4096), BF),
            ((128, 4096), BF),
            ((128, 448), F32),
        ]
        + shard
        + shard[:3]
        + [((4, 2, 8, 4096), BF), ((8, 4096), BF), ((8, 4096), BF)]
        + [((8, 4096), BF)] * 2
        + [((128, 448), BF)] * 3
        + [((448, 128), BF)] * 3
        + [((256, 128), BF)]
        + [((448, 1024), BF)] * 3
        + [((256, 1024), BF)]
        + [((8, 8, 512), BF)] * 3
        + [((8, 16, 8, 512), BF)] * 3
        + [
            ((128, 256), BF),
            ((8, 128, 256), BF),
            ((8, 128), F32),
            ((8, 8, 128), F32),
            ((16, 8, 256), F32),
            ((16, 8, 256), F32),
            ((1, 4096), F32),
            ((1, 4096), F32),
            ((8, 1, 4096), F32),
            ((1, 4096), F32),
            ((8, 1, 4096), F32),
        ]
    )
    shapes = [jax.ShapeDtypeStruct(s, d) for s, d in small + grads]
    results = pl.pallas_call(
        layer,
        out_shape=shapes,
        in_specs=[ANY] * 12,
        out_specs=[ANY] * len(shapes),
        scratch_shapes=[pltpu.VMEM(s, d) for s, d in scratch]
        + [pltpu.SemaphoreType.DMA((SEMS,)), pltpu.SemaphoreType.DMA((SEMS,))],
        compiler_params=pltpu.CompilerParams(
            collective_id=0, has_side_effects=True, vmem_limit_bytes=60 * 2**20
        ),
    )(
        keys_in, value_rows_input, queries, positions.reshape(1, 128), doc_ids.reshape(8, 128),
        resid_in, norm_gain.reshape(1, 4096), cotangent, w_out, w_gate.T, w_up.T, w_down,
    )
    mixed, gres, dq, kg, vg, gg, dwout, dwgate, dwup, dwdown = pl.pallas_call(
        hand_over,
        out_shape=shapes,
        in_specs=[ANY] * len(shapes),
        out_specs=[ANY] * len(shapes),
        scratch_shapes=[pltpu.VMEM(s, d) for s, d in small + grads]
        + [pltpu.SemaphoreType.DMA((len(shapes),))] * 2,
    )(*results)
    return (mixed, gres, dq, kg, vg, gg.reshape(4096), dwout, dwgate.T, dwup.T, dwdown)


def solution(mesh):
    rows = P(("ctx", "ffn"), None)
    return jax.shard_map(
        body,
        mesh=mesh,
        in_specs=(
            rows, P("ctx", "ffn"), P("ctx", None), P("ctx", None), P("ffn", None), P(),
            P(None, "ffn"), P(None, "ffn"), P("ffn", None), rows, P("ctx"), P(),
        ),
        out_specs=(
            rows, rows, P("ctx", "ffn"), rows, rows, P(), P("ffn", "ctx"), P("ctx", "ffn"),
            P("ctx", "ffn"), P("ffn", "ctx"),
        ),
        check_vma=False,
    )
```
